128 devices in a mesh: sky: 32 (over y, x, core), visit: 4 (over z).
Axes of the slice: x: 4, y: 4, z: 4, core: 2. Of those that a mesh axis runs over, the one named last changes fastest.
Arguments:
- images: bfloat16 [32, 3072, 2048], P('visit', 'sky'), may hold values from -6 to 6
- inv_var: bfloat16 [32, 3072, 2048], P('visit', 'sky'), may hold values from 0.25 to 4
- row_taps: bfloat16 [11, 41], replicated, may hold values from -1 to 1
- col_taps: bfloat16 [11, 41], replicated, may hold values from -1 to 1
- coeffs: float32 [32, 11, 3], replicated, may hold values from -4 to 4
- dithers: int32 [32], replicated, may hold values from 0 to 256, as said below
- depths: int32 [32], P('sky'), may hold values from 2 to 16, as said below
Outputs:
- coadd: float32 [3072, 2048], P('sky', 'visit')
The draws below stay inside these ranges and needn't reach their ends.
Inputs may be any that keep to these rules, and one draw needn't show every extreme that they name: `dithers`: some visit has offset 0 and some has offset 256. `depths`: some tile is covered by 16 visits.
All inputs are finite; a program needn't handle non-finite values.
Results may differ from the reference program's by a relative error of at most 0.0029.
Values may be sent and summed in bfloat16 or wider, within the bound.
No kernel may reach another device: no remote copies, remote signals or barrier semaphores. Data moves between devices by JAX's collectives and lax.ppermute only.
A program may use at most 64 MiB of HBM per device.

```python
import math
import jax
import jax.numpy as jnp
from jax import lax

ROWS = 96
NX = 2048
VISITS = 32
NB = 11
TAPS = 41
DEPTH_MAX = 16
DITHER = 256
TILES = 32
NY = 3072


def draw_dithers(key, part):
    drawn_vals = jax.random.randint(key, (VISITS,), 0, DITHER + 1)
    shuffled = jax.random.permutation(jax.random.fold_in(key, 5), VISITS)
    return drawn_vals.at[shuffled[0]].set(0).at[shuffled[1]].set(DITHER).astype(jnp.int32)


def draw_depths(key, part):
    drawn_vals = jax.random.randint(key, (TILES,), 0, DEPTH_MAX - 1)
    depth_vals = 2 + drawn_vals * drawn_vals // (DEPTH_MAX - 2)
    chosen = jax.random.randint(jax.random.fold_in(key, 11), (), 0, TILES)
    return depth_vals.at[chosen].set(DEPTH_MAX).astype(jnp.int32)


def levels(key, shape, split, least, top_value):
    factor_of, own = 1.0, jax.random.fold_in(key, 6)
    for axis_at, shards_of in split:
        draws = jnp.exp(jax.random.uniform(jax.random.fold_in(own, axis_at), (shards_of,), jnp.float32, least / len(split), top_value / len(split)))
        factor_of = factor_of * jnp.repeat(draws, shape[axis_at] // shards_of).reshape([-1 if axis == axis_at else 1 for axis in range(len(shape))])
    return factor_of


def normal_values(stream_key, extent, deviation, limit, shards=(), held_as=jnp.bfloat16):
    array = jax.random.normal(stream_key, extent, jnp.float32) * deviation
    if len(shards) > 0:
        array = levels(stream_key, extent, shards, -0.22, 0.18) * array
    return jnp.clip(array, min=-limit, max=limit).astype(held_as)


def setup_inputs(seed: int = 0) -> dict:
    key_list = jax.random.split(jax.random.key(seed), 8)
    images = normal_values(key_list[0], (VISITS, NY, NX), 1.0, 6.0, ((0, 4), (1, 32)))
    inv_var = jnp.clip(jnp.exp(math.log(4.0) - 2.7725887 * jax.random.uniform(key_list[1], (VISITS, NY, NX), jnp.float32) ** levels(key_list[1], (VISITS, NY, NX), ((0, 4), (1, 32)), -0.2, 0.2)), 0.25, 4.0).astype(jnp.bfloat16)
    row_taps = normal_values(key_list[2], (NB, TAPS), TAPS ** -0.5, 1.0)
    col_taps = normal_values(key_list[3], (NB, TAPS), TAPS ** -0.5, 1.0)
    coeffs = normal_values(key_list[4], (VISITS, NB, 3), 0.3, 4.0, (), jnp.float32)
    dithers = draw_dithers(jax.random.fold_in(key_list[7], 71), 0)
    depths = draw_depths(jax.random.fold_in(key_list[7], 71), 0)
    return {"images": images, "inv_var": inv_var, "row_taps": row_taps, "col_taps": col_taps, "coeffs": coeffs, "dithers": dithers, "depths": depths}


def reference(images, inv_var, row_taps, col_taps, coeffs, dithers, depths):
    half_taps = TAPS // 2
    row_kernel = row_taps.astype(jnp.float32)[:, None, :, None]
    col_kernel = col_taps.astype(jnp.float32)[:, None, None, :]
    col_ids = jnp.arange(NX, dtype=jnp.int32)
    row_ids = jnp.arange(NY, dtype=jnp.int32)
    col_coord = (2.0 * col_ids.astype(jnp.float32) + 1.0) / NX - 1.0
    row_coord = (2.0 * row_ids.astype(jnp.float32) + 1.0) / NY - 1.0
    tile_row = row_ids // ROWS
    first_visit = (tile_row * VISITS // TILES).astype(jnp.int32)
    row_depth = depths[tile_row]

    def one_visit(carry, visit):
        numerator, denominator = carry
        visit_plane = images[visit].astype(jnp.float32)[None, None]
        passed = lax.conv_general_dilated(visit_plane, row_kernel, (1, 1), ((half_taps, half_taps), (0, 0)), dimension_numbers=("NCHW", "OIHW", "NCHW"), precision=lax.Precision.HIGHEST)
        passed = lax.optimization_barrier(passed.astype(jnp.bfloat16)).astype(jnp.float32)
        basis_image = lax.conv_general_dilated(passed, col_kernel, (1, 1), ((0, 0), (half_taps, half_taps)), dimension_numbers=("NCHW", "OIHW", "NCHW"), feature_group_count=NB, precision=lax.Precision.HIGHEST)[0]
        coef_rows = coeffs[visit]
        spatial = coef_rows[:, 0, None, None] + coef_rows[:, 1, None, None] * col_coord[None, None, :] + coef_rows[:, 2, None, None] * row_coord[None, :, None]
        matched = jnp.sum(spatial * basis_image, axis=0)
        shift_cols = dithers[visit]
        inside = (col_ids >= shift_cols) & (col_ids < shift_cols + NX - DITHER)
        covered = jnp.mod(visit - first_visit, VISITS) < row_depth
        weight = inv_var[visit].astype(jnp.float32) * inside.astype(jnp.float32)[None, :] * covered.astype(jnp.float32)[:, None]
        return (numerator + weight * matched, denominator + weight), None

    starting = (jnp.zeros((NY, NX), jnp.float32), jnp.zeros((NY, NX), jnp.float32))
    (numerator, denominator), _ = lax.scan(one_visit, starting, jnp.arange(VISITS, dtype=jnp.int32))
    return numerator / (1.0 + denominator)
```

```python
import jax
import jax.numpy as jnp
from jax import lax
from jax.experimental import pallas as pl
from jax.experimental.pallas import tpu as pltpu
from jax.sharding import PartitionSpec as P

DITHER = 256
SIDE = 128
BLOCK = 256


def row_table(row_taps, row_count):
    basis_count, tap_count = row_taps.shape
    half = tap_count // 2
    slot = jnp.arange(row_count + 64, dtype=jnp.int32)
    top_row = jnp.where(slot < row_count + half, slot - row_count - half, 9999)
    bottom_row = jnp.where(slot < row_count + 32 + half, slot - 32, 9999)
    source = jnp.where(
        slot < row_count, slot, jnp.where(slot < row_count + 32, top_row, bottom_row)
    )
    offset = source[None, :] - jnp.arange(row_count, dtype=jnp.int32)[:, None] + half
    picks = (offset[None] == jnp.arange(tap_count, dtype=jnp.int32)[:, None, None]).astype(
        jnp.bfloat16
    )
    table = jnp.einsum("kt,tos->kos", row_taps, picks, preferred_element_type=jnp.float32)
    return table.astype(jnp.bfloat16).reshape(basis_count * row_count, row_count + 64)


def col_table(col_taps):
    tap_count = col_taps.shape[1]
    half = tap_count // 2
    offset = (
        jnp.arange(BLOCK + 2 * SIDE, dtype=jnp.int32)[:, None]
        - SIDE
        + half
        - jnp.arange(BLOCK, dtype=jnp.int32)[None, :]
    )
    picks = (offset[None] == jnp.arange(tap_count, dtype=jnp.int32)[:, None, None]).astype(
        jnp.bfloat16
    )
    table = jnp.einsum("kt,tpx->kpx", col_taps, picks, preferred_element_type=jnp.float32)
    return table.astype(jnp.bfloat16)


def coadd_kernel(
    scalars,
    coeffs,
    images,
    top,
    bottom,
    inv_var,
    rows_ref,
    cols_ref,
    num_ref,
    den_ref,
    source,
    passed,
    matched,
    *,
    total_rows,
):
    visit = pl.program_id(0)
    visit_count = pl.num_programs(0)
    row_count, col_count = num_ref.shape
    basis_count = cols_ref.shape[0]
    half = top.shape[1]
    blocks = col_count // BLOCK
    row_first = scalars[0]

    @pl.when(visit == 0)
    def _():
        source[...] = jnp.zeros_like(source)
        passed[...] = jnp.zeros_like(passed)
        num_ref[...] = jnp.zeros_like(num_ref)
        den_ref[...] = jnp.zeros_like(den_ref)

    covered = scalars[1 + visit]
    shift = scalars[1 + visit_count + visit]

    @pl.when(covered > 0)
    def _():
        source[0:row_count, :] = images[0]
        source[row_count : row_count + half, :] = top[0]
        source[row_count + 32 : row_count + 32 + half, :] = bottom[0]

        def row_step(block, carry):
            at = pl.multiple_of(block * BLOCK, BLOCK)
            out = jnp.dot(
                rows_ref[...], source[:, pl.ds(at, BLOCK)], preferred_element_type=jnp.float32
            )
            passed[:, pl.ds(pl.multiple_of(at + SIDE, SIDE), BLOCK)] = out.astype(jnp.bfloat16)
            return carry

        lax.fori_loop(0, blocks, row_step, 0)
        matched[...] = jnp.zeros_like(matched)
        row_ids = row_first + lax.broadcasted_iota(jnp.int32, (row_count, 128), 0)
        row_coord = (2.0 * row_ids.astype(jnp.float32) + 1.0) / total_rows - 1.0
        col_ids = lax.broadcasted_iota(jnp.int32, (8, col_count), 1)
        col_coord = (2.0 * col_ids.astype(jnp.float32) + 1.0) / col_count - 1.0

        def col_step(basis, carry):
            first = pl.multiple_of(basis * row_count, row_count)
            lhs = jnp.concatenate(
                [
                    passed[pl.ds(first, row_count), b * BLOCK : (b + 2) * BLOCK]
                    for b in range(blocks)
                ],
                axis=0,
            )
            image = jnp.dot(lhs, cols_ref[basis], preferred_element_type=jnp.float32)
            at = (visit * basis_count + basis) * 3
            row_part = coeffs[at] + coeffs[at + 2] * row_coord
            row_part = jnp.concatenate([row_part, row_part], axis=1)
            col_part = coeffs[at + 1] * col_coord
            for b in range(blocks):
                spatial = row_part.reshape(row_count // 8, 8, BLOCK) + col_part[
                    None, :, b * BLOCK : (b + 1) * BLOCK
                ]
                matched[:, b * BLOCK : (b + 1) * BLOCK] += (
                    spatial.reshape(row_count, BLOCK) * image[b * row_count : (b + 1) * row_count]
                )
            return carry

        lax.fori_loop(0, basis_count, col_step, 0)
        inside = (col_ids[0:1] >= shift) & (col_ids[0:1] < shift + (col_count - DITHER))
        weight = inv_var[0].astype(jnp.float32) * inside.astype(jnp.float32)
        num_ref[...] += weight * matched[...]
        den_ref[...] += weight


def partial_sums(scalars, coeffs, images, top, bottom, inv_var, rows, cols, total_rows):
    visit_count, row_count, col_count = images.shape
    half = top.shape[1]
    plane = jax.ShapeDtypeStruct((row_count, col_count), jnp.float32)
    whole = lambda shape: pl.BlockSpec(shape, lambda v, *_: (0,) * len(shape))
    return pl.pallas_call(
        lambda *refs: coadd_kernel(*refs, total_rows=total_rows),
        out_shape=(plane, plane),
        grid_spec=pltpu.PrefetchScalarGridSpec(
            num_scalar_prefetch=2,
            grid=(visit_count,),
            in_specs=[
                pl.BlockSpec((1, row_count, col_count), lambda v, *_: (v, 0, 0)),
                pl.BlockSpec((1, half, col_count), lambda v, *_: (v, 0, 0)),
                pl.BlockSpec((1, half, col_count), lambda v, *_: (v, 0, 0)),
                pl.BlockSpec((1, row_count, col_count), lambda v, *_: (v, 0, 0)),
                whole(rows.shape),
                whole(cols.shape),
            ],
            out_specs=[whole((row_count, col_count))] * 2,
            scratch_shapes=[
                pltpu.VMEM((row_count + 64, col_count), jnp.bfloat16),
                pltpu.VMEM((rows.shape[0], col_count + 2 * SIDE), jnp.bfloat16),
                pltpu.VMEM((row_count, col_count), jnp.float32),
            ],
        ),
        compiler_params=pltpu.CompilerParams(
            dimension_semantics=("arbitrary",), vmem_limit_bytes=60 << 20
        ),
        name="coadd",
    )(scalars, coeffs, images, top, bottom, inv_var, rows, cols)


def local(images, inv_var, row_taps, col_taps, coeffs, dithers, depths):
    visit_count, row_count, col_count = images.shape
    half = row_taps.shape[1] // 2
    sky = lax.axis_index("sky")
    tiles = lax.axis_size("sky")
    group = lax.axis_index("visit")
    visits_all = visit_count * lax.axis_size("visit")
    top = lax.ppermute(
        images[:, row_count - half :], "sky", [(i, i + 1) for i in range(tiles - 1)]
    )
    bottom = lax.ppermute(images[:, :half], "sky", [(i + 1, i) for i in range(tiles - 1)])
    order = group * visit_count + jnp.arange(visit_count, dtype=jnp.int32)
    covered = jnp.mod(order - sky * visits_all // tiles, visits_all) < depths[0]
    shifts = lax.dynamic_slice_in_dim(dithers, group * visit_count, visit_count, 0)
    scalars = jnp.concatenate(
        [(sky * row_count)[None].astype(jnp.int32), covered.astype(jnp.int32), shifts]
    )
    coefs = lax.dynamic_slice_in_dim(coeffs, group * visit_count, visit_count, 0).reshape(-1)
    numerator, denominator = partial_sums(
        scalars,
        coefs,
        images,
        top,
        bottom,
        inv_var,
        row_table(row_taps, row_count),
        col_table(col_taps),
        row_count * tiles,
    )
    numerator = lax.psum_scatter(numerator, "visit", scatter_dimension=1, tiled=True)
    denominator = lax.psum_scatter(denominator, "visit", scatter_dimension=1, tiled=True)
    return numerator / (1.0 + denominator)


def solution(mesh):
    placed = (P("visit", "sky", None), P("visit", "sky", None), P(), P(), P(), P(), P("sky"))
    return jax.shard_map(
        local, mesh=mesh, in_specs=placed, out_specs=P("sky", "visit"), check_vma=False
    )
```

```python
import jax
import jax.numpy as jnp
from jax import lax
from jax.experimental import pallas as pl
from jax.experimental.pallas import tpu as pltpu
from jax.sharding import PartitionSpec as P

DITHER = 256
SIDE = 128
BLOCK = 256


def row_table(row_taps, row_count):
    basis_count, tap_count = row_taps.shape
    half = tap_count // 2
    slot = jnp.arange(row_count + 64, dtype=jnp.int32)
    top_row = jnp.where(slot < row_count + half, slot - row_count - half, 9999)
    bottom_row = jnp.where(slot < row_count + 32 + half, slot - 32, 9999)
    source = jnp.where(
        slot < row_count, slot, jnp.where(slot < row_count + 32, top_row, bottom_row)
    )
    offset = source[None, :] - jnp.arange(row_count, dtype=jnp.int32)[:, None] + half
    picks = (offset[None] == jnp.arange(tap_count, dtype=jnp.int32)[:, None, None]).astype(
        jnp.bfloat16
    )
    table = jnp.einsum("kt,tos->kos", row_taps, picks, preferred_element_type=jnp.float32)
    return table.astype(jnp.bfloat16).reshape(basis_count * row_count, row_count + 64)


def col_table(col_taps):
    tap_count = col_taps.shape[1]
    half = tap_count // 2
    offset = (
        jnp.arange(BLOCK + 2 * SIDE, dtype=jnp.int32)[:, None]
        - SIDE
        + half
        - jnp.arange(BLOCK, dtype=jnp.int32)[None, :]
    )
    picks = (offset[None] == jnp.arange(tap_count, dtype=jnp.int32)[:, None, None]).astype(
        jnp.bfloat16
    )
    table = jnp.einsum("kt,tpx->kpx", col_taps, picks, preferred_element_type=jnp.float32)
    return table.astype(jnp.bfloat16)


def coadd_kernel(
    scalars,
    coeffs,
    images,
    top,
    bottom,
    inv_var,
    rows_ref,
    cols_ref,
    own_ref,
    send_ref,
    source,
    passed,
    matched,
    num_ref,
    *,
    total_rows,
):
    visit = pl.program_id(0)
    visit_count = pl.num_programs(0)
    row_count, col_count = num_ref.shape
    basis_count = cols_ref.shape[0]
    half = top.shape[1]
    blocks = col_count // BLOCK
    row_first = scalars[0]

    @pl.when(visit == 0)
    def _():
        source[...] = jnp.zeros_like(source)
        passed[...] = jnp.zeros_like(passed)
        num_ref[...] = jnp.zeros_like(num_ref)

    covered = scalars[1 + visit]
    shift = scalars[1 + visit_count + visit]

    @pl.when(covered > 0)
    def _():
        source[0:row_count, :] = images[0]
        source[row_count : row_count + half, :] = top[0]
        source[row_count + 32 : row_count + 32 + half, :] = bottom[0]

        def row_step(block, carry):
            at = pl.multiple_of(block * BLOCK, BLOCK)
            out = jnp.dot(
                rows_ref[...], source[:, pl.ds(at, BLOCK)], preferred_element_type=jnp.float32
            )
            passed[:, pl.ds(pl.multiple_of(at + SIDE, SIDE), BLOCK)] = out.astype(jnp.bfloat16)
            return carry

        lax.fori_loop(0, blocks, row_step, 0)
        matched[...] = jnp.zeros_like(matched)
        row_ids = row_first + lax.broadcasted_iota(jnp.int32, (row_count, 128), 0)
        row_coord = (2.0 * row_ids.astype(jnp.float32) + 1.0) / total_rows - 1.0
        col_ids = lax.broadcasted_iota(jnp.int32, (8, col_count), 1)
        col_coord = (2.0 * col_ids.astype(jnp.float32) + 1.0) / col_count - 1.0

        def col_step(basis, carry):
            first = pl.multiple_of(basis * row_count, row_count)
            lhs = jnp.concatenate(
                [
                    passed[pl.ds(first, row_count), b * BLOCK : (b + 2) * BLOCK]
                    for b in range(blocks)
                ],
                axis=0,
            )
            image = jnp.dot(lhs, cols_ref[basis], preferred_element_type=jnp.float32)
            at = (visit * basis_count + basis) * 3
            row_part = coeffs[at] + coeffs[at + 2] * row_coord
            row_part = jnp.concatenate([row_part, row_part], axis=1)
            col_part = coeffs[at + 1] * col_coord
            for b in range(blocks):
                spatial = row_part.reshape(row_count // 8, 8, BLOCK) + col_part[
                    None, :, b * BLOCK : (b + 1) * BLOCK
                ]
                matched[:, b * BLOCK : (b + 1) * BLOCK] += (
                    spatial.reshape(row_count, BLOCK) * image[b * row_count : (b + 1) * row_count]
                )
            return carry

        lax.fori_loop(0, basis_count, col_step, 0)
        inside = (col_ids[0:1] >= shift) & (col_ids[0:1] < shift + (col_count - DITHER))
        weight = inv_var[0].astype(jnp.float32) * inside.astype(jnp.float32)
        num_ref[...] += weight * matched[...]

    @pl.when(visit == visit_count - 1)
    def _():
        split_strips(scalars[1 + 2 * visit_count], num_ref, own_ref, send_ref)


def split_strips(group, total, own_ref, send_ref):
    groups = send_ref.shape[0] + 1
    width = own_ref.shape[1]
    for ahead in range(groups):
        at = pl.multiple_of(lax.rem(group + ahead, groups) * width, width)
        strip = total[:, pl.ds(at, width)]
        if ahead == 0:
            own_ref[...] = strip
        else:
            send_ref[ahead - 1] = strip.astype(jnp.bfloat16)


def weight_kernel(scalars, inv_var, own_ref, send_ref, den_ref):
    visit_count, row_count, col_count = inv_var.shape
    col_ids = lax.broadcasted_iota(jnp.int32, (1, col_count), 1)
    den_ref[...] = jnp.zeros_like(den_ref)

    def step(visit, carry):
        shift = scalars[1 + visit_count + visit]

        @pl.when(scalars[1 + visit] > 0)
        def _():
            inside = (col_ids >= shift) & (col_ids < shift + (col_count - DITHER))
            den_ref[...] += inv_var[visit].astype(jnp.float32) * inside.astype(jnp.float32)

        return carry

    lax.fori_loop(0, visit_count, step, 0)
    split_strips(scalars[1 + 2 * visit_count], den_ref, own_ref, send_ref)


def strip_shapes(row_count, col_count, groups):
    width = col_count // groups
    return (
        jax.ShapeDtypeStruct((row_count, width), jnp.float32),
        jax.ShapeDtypeStruct((groups - 1, row_count, width), jnp.bfloat16),
    )


def weight_sums(scalars, inv_var, groups):
    visit_count, row_count, col_count = inv_var.shape
    return pl.pallas_call(
        weight_kernel,
        out_shape=strip_shapes(row_count, col_count, groups),
        in_specs=[
            pl.BlockSpec(memory_space=pltpu.SMEM),
            pl.BlockSpec(memory_space=pltpu.VMEM),
        ],
        out_specs=[pl.BlockSpec(memory_space=pltpu.VMEM)] * 2,
        scratch_shapes=[pltpu.VMEM((row_count, col_count), jnp.float32)],
        name="weights",
    )(scalars, inv_var)


def exchange(own, sends, axis):
    groups = sends.shape[0] + 1
    for ahead in range(1, groups):
        got = lax.ppermute(
            sends[ahead - 1], axis, [(i, (i + ahead) % groups) for i in range(groups)]
        )
        own = own + got.astype(jnp.float32)
    return own


def partial_sums(scalars, coeffs, images, top, bottom, inv_var, rows, cols, total_rows, groups):
    visit_count, row_count, col_count = images.shape
    half = top.shape[1]
    shapes = strip_shapes(row_count, col_count, groups)
    whole = lambda shape: pl.BlockSpec(shape, lambda v, *_: (0,) * len(shape))
    return pl.pallas_call(
        lambda *refs: coadd_kernel(*refs, total_rows=total_rows),
        out_shape=shapes,
        grid_spec=pltpu.PrefetchScalarGridSpec(
            num_scalar_prefetch=2,
            grid=(visit_count,),
            in_specs=[
                pl.BlockSpec((1, row_count, col_count), lambda v, *_: (v, 0, 0)),
                pl.BlockSpec((1, half, col_count), lambda v, *_: (v, 0, 0)),
                pl.BlockSpec((1, half, col_count), lambda v, *_: (v, 0, 0)),
                pl.BlockSpec((1, row_count, col_count), lambda v, *_: (v, 0, 0)),
                whole(rows.shape),
                whole(cols.shape),
            ],
            out_specs=[whole(shape.shape) for shape in shapes],
            scratch_shapes=[
                pltpu.VMEM((row_count + 64, col_count), jnp.bfloat16),
                pltpu.VMEM((rows.shape[0], col_count + 2 * SIDE), jnp.bfloat16),
                pltpu.VMEM((row_count, col_count), jnp.float32),
                pltpu.VMEM((row_count, col_count), jnp.float32),
            ],
        ),
        compiler_params=pltpu.CompilerParams(
            dimension_semantics=("arbitrary",), vmem_limit_bytes=60 << 20
        ),
        name="coadd",
    )(scalars, coeffs, images, top, bottom, inv_var, rows, cols)


def local(images, inv_var, row_taps, col_taps, coeffs, dithers, depths):
    visit_count, row_count, col_count = images.shape
    half = row_taps.shape[1] // 2
    sky = lax.axis_index("sky")
    tiles = lax.axis_size("sky")
    group = lax.axis_index("visit")
    groups = lax.axis_size("visit")
    visits_all = visit_count * groups
    top = lax.ppermute(
        images[:, row_count - half :], "sky", [(i, i + 1) for i in range(tiles - 1)]
    )
    bottom = lax.ppermute(images[:, :half], "sky", [(i + 1, i) for i in range(tiles - 1)])
    order = group * visit_count + jnp.arange(visit_count, dtype=jnp.int32)
    covered = jnp.mod(order - sky * visits_all // tiles, visits_all) < depths[0]
    shifts = lax.dynamic_slice_in_dim(dithers, group * visit_count, visit_count, 0)
    scalars = jnp.concatenate(
        [(sky * row_count)[None], covered.astype(jnp.int32), shifts, group[None]]
    )
    den_own, den_sends = weight_sums(scalars, inv_var, groups)
    denominator = exchange(den_own, den_sends, "visit")
    coefs = lax.dynamic_slice_in_dim(coeffs, group * visit_count, visit_count, 0).reshape(-1)
    num_own, num_sends = partial_sums(
        scalars,
        coefs,
        images,
        top,
        bottom,
        inv_var,
        row_table(row_taps, row_count),
        col_table(col_taps),
        row_count * tiles,
        groups,
    )
    numerator = exchange(num_own, num_sends, "visit")
    return numerator / (1.0 + denominator)


def solution(mesh):
    placed = (P("visit", "sky", None), P("visit", "sky", None), P(), P(), P(), P(), P("sky"))
    return jax.shard_map(
        local, mesh=mesh, in_specs=placed, out_specs=P("sky", "visit"), check_vma=False
    )
```

```python
import jax
import jax.numpy as jnp
from jax import lax
from jax.experimental import pallas as pl
from jax.experimental.pallas import tpu as pltpu
from jax.sharding import PartitionSpec as P

DITHER = 256
SIDE = 128
BLOCK = 256
HALO = 32


def tap_rows(row_taps, col_taps):
    tap_count = row_taps.shape[1]
    half = tap_count // 2
    row_base = jnp.pad(row_taps, ((0, 0), (HALO - half, 256 - tap_count - HALO + half)))
    col_base = jnp.pad(col_taps[:, ::-1], ((0, 0), (SIDE - half, 512 - tap_count - SIDE + half)))
    return row_base.astype(jnp.float32), col_base.astype(jnp.float32)


def build_tables(row_base, col_base, rows_ref, cols_ref):
    basis_count = col_base.shape[0]
    row_count = rows_ref.shape[0] // basis_count
    nothing = jnp.zeros((128, 128), jnp.bfloat16)

    def step(basis, carry):
        wide = jnp.broadcast_to(row_base[pl.ds(basis, 1), :], (row_count, 256))
        wide = pltpu.roll(wide, 0, 1, stride=1, stride_axis=0).astype(jnp.bfloat16)
        at = pl.multiple_of(basis * row_count, row_count)
        rows_ref[pl.ds(at, row_count), :] = wide[:, : rows_ref.shape[1]]
        band = jnp.broadcast_to(col_base[pl.ds(basis, 1), :], (128, 512))
        band = pltpu.roll(band, 0, 1, stride=1, stride_axis=0).astype(jnp.bfloat16)
        for p in range(cols_ref.shape[1] // 128):
            for x in range(cols_ref.shape[2] // 128):
                apart = p - x
                piece = band[:, (2 - apart) * 128 : (3 - apart) * 128] if 0 <= apart < 3 else nothing
                cols_ref[basis, p * 128 : (p + 1) * 128, x * 128 : (x + 1) * 128] = piece
        return carry

    lax.fori_loop(0, basis_count, step, 0)


def coadd_kernel(
    scalars,
    coeffs,
    images,
    top,
    bottom,
    inv_var,
    row_base,
    col_base,
    own_ref,
    *rest,
    total_rows,
):
    send_refs = rest[:-6]
    source, passed, matched, num_ref, rows_ref, cols_ref = rest[-6:]
    visit = pl.program_id(0)
    visit_count = pl.num_programs(0)
    row_count, col_count = num_ref.shape
    basis_count = cols_ref.shape[0]
    half = top.shape[1]
    blocks = col_count // BLOCK
    row_first = scalars[0]

    @pl.when(visit == 0)
    def _():
        source[...] = jnp.zeros_like(source)
        passed[...] = jnp.zeros_like(passed)
        build_tables(row_base, col_base, rows_ref, cols_ref)
        num_ref[...] = jnp.zeros_like(num_ref)

    covered = scalars[1 + visit]
    shift = scalars[1 + visit_count + visit]

    @pl.when(covered > 0)
    def _():
        source[HALO - half : HALO, :] = top[0]
        source[HALO : HALO + row_count, :] = images[0]
        source[HALO + row_count : HALO + row_count + half, :] = bottom[0]

        def row_step(block, carry):
            at = pl.multiple_of(block * BLOCK, BLOCK)
            out = jnp.dot(
                rows_ref[...], source[:, pl.ds(at, BLOCK)], preferred_element_type=jnp.float32
            )
            passed[:, pl.ds(pl.multiple_of(at + SIDE, SIDE), BLOCK)] = out.astype(jnp.bfloat16)
            return carry

        lax.fori_loop(0, blocks, row_step, 0, unroll=True)
        matched[...] = jnp.zeros_like(matched)
        row_ids = row_first + lax.broadcasted_iota(jnp.int32, (row_count, 128), 0)
        row_coord = (2.0 * row_ids.astype(jnp.float32) + 1.0) / total_rows - 1.0
        col_ids = lax.broadcasted_iota(jnp.int32, (8, col_count), 1)
        col_coord = (2.0 * col_ids.astype(jnp.float32) + 1.0) / col_count - 1.0

        def col_step(basis, carry):
            first = pl.multiple_of(basis * row_count, row_count)
            lhs = jnp.concatenate(
                [
                    passed[pl.ds(first, row_count), b * BLOCK : (b + 2) * BLOCK]
                    for b in range(blocks)
                ],
                axis=0,
            )
            image = jnp.dot(lhs, cols_ref[basis], preferred_element_type=jnp.float32)
            at = (visit * basis_count + basis) * 3
            row_part = coeffs[at] + coeffs[at + 2] * row_coord
            row_part = jnp.concatenate([row_part, row_part], axis=1)
            col_part = coeffs[at + 1] * col_coord
            for b in range(blocks):
                spatial = row_part.reshape(row_count // 8, 8, BLOCK) + col_part[
                    None, :, b * BLOCK : (b + 1) * BLOCK
                ]
                matched[:, b * BLOCK : (b + 1) * BLOCK] += (
                    spatial.reshape(row_count, BLOCK) * image[b * row_count : (b + 1) * row_count]
                )
            return carry

        lax.fori_loop(0, basis_count, col_step, 0, unroll=True)
        inside = (col_ids[0:1] >= shift) & (col_ids[0:1] < shift + (col_count - DITHER))
        weight = inv_var[0].astype(jnp.float32) * inside.astype(jnp.float32)
        num_ref[...] += weight * matched[...]

    @pl.when(visit == visit_count - 1)
    def _():
        split_strips(scalars[1 + 2 * visit_count], num_ref, own_ref, send_refs)


def split_strips(group, total, own_ref, send_refs):
    groups = len(send_refs) + 1
    width = own_ref.shape[1]
    for ahead in range(groups):
        at = pl.multiple_of(lax.rem(group + ahead, groups) * width, width)
        strip = total[:, pl.ds(at, width)]
        if ahead == 0:
            own_ref[...] = strip
        else:
            send_refs[ahead - 1][...] = strip.astype(jnp.bfloat16)


def weight_kernel(scalars, inv_var, own_ref, *rest):
    send_refs, den_ref = rest[:-1], rest[-1]
    visit_count, row_count, col_count = inv_var.shape
    col_ids = lax.broadcasted_iota(jnp.int32, (1, col_count), 1)
    den_ref[...] = jnp.zeros_like(den_ref)

    def step(visit, carry):
        shift = scalars[1 + visit_count + visit]

        @pl.when(scalars[1 + visit] > 0)
        def _():
            inside = (col_ids >= shift) & (col_ids < shift + (col_count - DITHER))
            den_ref[...] += inv_var[visit].astype(jnp.float32) * inside.astype(jnp.float32)

        return carry

    lax.fori_loop(0, visit_count, step, 0)
    split_strips(scalars[1 + 2 * visit_count], den_ref, own_ref, send_refs)


def strip_shapes(row_count, col_count, groups):
    width = col_count // groups
    return (
        jax.ShapeDtypeStruct((row_count, width), jnp.float32),
    ) + (jax.ShapeDtypeStruct((row_count, width), jnp.bfloat16),) * (groups - 1)


def weight_sums(scalars, inv_var, groups):
    visit_count, row_count, col_count = inv_var.shape
    return pl.pallas_call(
        weight_kernel,
        out_shape=strip_shapes(row_count, col_count, groups),
        in_specs=[
            pl.BlockSpec(memory_space=pltpu.SMEM),
            pl.BlockSpec(memory_space=pltpu.VMEM),
        ],
        out_specs=[pl.BlockSpec(memory_space=pltpu.VMEM)] * groups,
        scratch_shapes=[pltpu.VMEM((row_count, col_count), jnp.float32)],
        name="weights",
    )(scalars, inv_var)


def exchange(own, sends, axis):
    groups = len(sends) + 1
    for ahead in range(1, groups):
        got = lax.ppermute(
            sends[ahead - 1], axis, [(i, (i + ahead) % groups) for i in range(groups)]
        )
        own = own + got.astype(jnp.float32)
    return own


def partial_sums(scalars, coeffs, images, top, bottom, inv_var, rows, cols, total_rows, groups):
    visit_count, row_count, col_count = images.shape
    half = top.shape[1]
    shapes = strip_shapes(row_count, col_count, groups)
    whole = lambda shape: pl.BlockSpec(shape, lambda v, *_: (0,) * len(shape))
    return pl.pallas_call(
        lambda *refs: coadd_kernel(*refs, total_rows=total_rows),
        out_shape=shapes,
        grid_spec=pltpu.PrefetchScalarGridSpec(
            num_scalar_prefetch=2,
            grid=(visit_count,),
            in_specs=[
                pl.BlockSpec((1, row_count, col_count), lambda v, *_: (v, 0, 0)),
                pl.BlockSpec((1, half, col_count), lambda v, *_: (v, 0, 0)),
                pl.BlockSpec((1, half, col_count), lambda v, *_: (v, 0, 0)),
                pl.BlockSpec((1, row_count, col_count), lambda v, *_: (v, 0, 0)),
                whole(rows.shape),
                whole(cols.shape),
            ],
            out_specs=[whole(shape.shape) for shape in shapes],
            scratch_shapes=[
                pltpu.VMEM((row_count + 2 * HALO, col_count), jnp.bfloat16),
                pltpu.VMEM((rows.shape[0] * row_count, col_count + 2 * SIDE), jnp.bfloat16),
                pltpu.VMEM((row_count, col_count), jnp.float32),
                pltpu.VMEM((row_count, col_count), jnp.float32),
                pltpu.VMEM((rows.shape[0] * row_count, row_count + 2 * HALO), jnp.bfloat16),
                pltpu.VMEM((rows.shape[0], BLOCK + 2 * SIDE, BLOCK), jnp.bfloat16),
            ],
        ),
        compiler_params=pltpu.CompilerParams(
            dimension_semantics=("arbitrary",), vmem_limit_bytes=60 << 20
        ),
        name="coadd",
    )(scalars, coeffs, images, top, bottom, inv_var, rows, cols)


def local(images, inv_var, row_taps, col_taps, coeffs, dithers, depths):
    visit_count, row_count, col_count = images.shape
    half = -(-(row_taps.shape[1] // 2) // 8) * 8
    sky = lax.axis_index("sky")
    tiles = lax.axis_size("sky")
    group = lax.axis_index("visit")
    groups = lax.axis_size("visit")
    visits_all = visit_count * groups
    top = lax.ppermute(
        images[:, row_count - half :], "sky", [(i, i + 1) for i in range(tiles - 1)]
    )
    bottom = lax.ppermute(images[:, :half], "sky", [(i + 1, i) for i in range(tiles - 1)])
    order = group * visit_count + jnp.arange(visit_count, dtype=jnp.int32)
    covered = jnp.mod(order - sky * visits_all // tiles, visits_all) < depths[0]
    shifts = lax.dynamic_slice_in_dim(dithers, group * visit_count, visit_count, 0)
    scalars = jnp.concatenate(
        [(sky * row_count)[None], covered.astype(jnp.int32), shifts, group[None]]
    )
    den_own, *den_sends = weight_sums(scalars, inv_var, groups)
    denominator = exchange(den_own, den_sends, "visit")
    coefs = lax.dynamic_slice_in_dim(coeffs, group * visit_count, visit_count, 0).reshape(-1)
    num_own, *num_sends = partial_sums(
        scalars,
        coefs,
        images,
        top,
        bottom,
        inv_var,
        *tap_rows(row_taps, col_taps),
        row_count * tiles,
        groups,
    )
    numerator = exchange(num_own, num_sends, "visit")
    return numerator / (1.0 + denominator)


def solution(mesh):
    placed = (P("visit", "sky", None), P("visit", "sky", None), P(), P(), P(), P(), P("sky"))
    return jax.shard_map(
        local, mesh=mesh, in_specs=placed, out_specs=P("sky", "visit"), check_vma=False
    )
```

```python
import jax
import jax.numpy as jnp
from jax import lax
from jax.experimental import pallas as pl
from jax.experimental.pallas import tpu as pltpu
from jax.sharding import PartitionSpec as P

DITHER = 256
SIDE = 128
BLOCK = 256
HALO = 32
INNER = 24


def put_columns(cols_ref, basis, band, nothing):
    for p in range(cols_ref.shape[1] // 128):
        for x in range(cols_ref.shape[2] // 128):
            apart = p - x
            piece = band[apart * 128 : (apart + 1) * 128, :] if 0 <= apart < 3 else nothing
            cols_ref[basis, p * 128 : (p + 1) * 128, x * 128 : (x + 1) * 128] = piece


def build_tables(row_taps, col_taps, rows_ref, cols_ref, laid, row_count, above, runs):
    basis_count, tap_count = row_taps.shape
    half = tap_count // 2
    kept = rows_ref.shape[0] // basis_count
    nothing = jnp.zeros((128, 128), jnp.bfloat16)
    laid[...] = jnp.zeros_like(laid)
    laid[0, 0:basis_count, 0:tap_count] = row_taps[...].astype(jnp.float32)
    laid[1, 0:basis_count, 0:tap_count] = col_taps[...].astype(jnp.float32)
    laid[0, :, 0:256] = pltpu.roll(laid[0, :, 0:256], (above - half) % 256, 1)
    laid[1] = pltpu.roll(laid[1], SIDE - half, 1)

    def step(basis, carry):
        wide = jnp.broadcast_to(laid[0, pl.ds(basis, 1), 0:256], (row_count, 256))
        wide = pltpu.roll(wide, 0, 1, stride=1, stride_axis=0)
        wide = jnp.concatenate([wide[first:last] for first, last in runs], axis=0)
        at = pl.multiple_of(basis * kept, kept)
        rows_ref[pl.ds(at, kept), :] = wide[:, : rows_ref.shape[1]].astype(jnp.bfloat16)
        band = jnp.broadcast_to(laid[1, pl.ds(basis, 1), :], (128, 512))
        band = pltpu.roll(band, 0, 1, stride=1, stride_axis=0)[:, :384]
        put_columns(cols_ref, basis, jnp.transpose(band).astype(jnp.bfloat16), nothing)
        return carry

    lax.fori_loop(0, basis_count, step, 0)


def split_strips(total, out_refs):
    groups = len(out_refs)
    width = out_refs[0].shape[1]
    group = lax.axis_index("visit")
    for ahead, out_ref in enumerate(out_refs):
        at = pl.multiple_of(lax.rem(group + ahead, groups) * width, width)
        out_ref[...] = total[:, pl.ds(at, width)].astype(out_ref.dtype)


def coadd_kernel(dithers, depths, coeffs, row_taps, col_taps, images, inv_var, *rest, total_rows, tiles, edges, groups):
    visit = pl.program_id(0)
    visit_count = pl.num_programs(0)
    row_count, col_count = images.shape[1:]
    basis_count = row_taps.shape[0]
    blocks = col_count // BLOCK
    visits_all = dithers.shape[0]
    sky = lax.axis_index("sky")
    order = lax.axis_index("visit") * visit_count + visit
    covered = lax.rem(order - sky * visits_all // tiles + visits_all, visits_all) < depths[0]
    if edges:
        top, bottom, inner = rest[:3]
        outs, (rows_ref, cols_ref, laid, passed, matched, num_ref, source) = (
            rest[3 : 3 + groups],
            rest[3 + groups :],
        )
        runs = ((0, INNER), (row_count - INNER, row_count))
        above = HALO
    else:
        inner_ref = rest[0]
        outs, (rows_ref, cols_ref, laid, passed, matched, num_ref, den_ref) = (
            rest[1 : 1 + groups],
            rest[1 + groups :],
        )
        runs = ((INNER, row_count - INNER),)
        above = 0
    kept = sum(last - first for first, last in runs)

    def pick(value):
        return jnp.concatenate([value[first:last] for first, last in runs], axis=0)

    @pl.when(visit == 0)
    def _():
        passed[:, 0:SIDE] = jnp.zeros((passed.shape[0], SIDE), jnp.bfloat16)
        passed[:, SIDE + col_count :] = jnp.zeros((passed.shape[0], SIDE), jnp.bfloat16)
        build_tables(row_taps, col_taps, rows_ref, cols_ref, laid, row_count, above, runs)
        num_ref[...] = jnp.zeros_like(num_ref)
        if edges:
            source[...] = jnp.zeros_like(source)
        else:
            den_ref[...] = jnp.zeros_like(den_ref)

    @pl.when(covered)
    def _():
        if edges:
            half = top.shape[1]
            source[HALO - half : HALO, :] = top[0]
            source[HALO : HALO + row_count, :] = images[0]
            source[HALO + row_count : HALO + row_count + half, :] = bottom[0]
        for b in range(blocks):
            piece = slice(b * BLOCK, (b + 1) * BLOCK)
            data = source[:, piece] if edges else images[0, :, piece]
            out = jnp.dot(rows_ref[...], data, preferred_element_type=jnp.float32)
            passed[:, SIDE + b * BLOCK : SIDE + (b + 1) * BLOCK] = out.astype(jnp.bfloat16)
        row_ids = sky * row_count + lax.broadcasted_iota(jnp.int32, (row_count, 128), 0)
        row_coord = pick((2.0 * row_ids.astype(jnp.float32) + 1.0) / total_rows - 1.0)
        col_ids = lax.broadcasted_iota(jnp.int32, (8, col_count), 1)
        col_coord = (2.0 * col_ids.astype(jnp.float32) + 1.0) / col_count - 1.0
        for basis in range(basis_count):
            band = slice(basis * kept, (basis + 1) * kept)
            lhs = jnp.concatenate(
                [passed[band, b * BLOCK : (b + 2) * BLOCK] for b in range(blocks)], axis=0
            )
            image = jnp.dot(lhs, cols_ref[basis], preferred_element_type=jnp.float32)
            row_part = coeffs[order, basis, 0] + coeffs[order, basis, 2] * row_coord
            row_part = jnp.concatenate([row_part, row_part], axis=1)
            col_part = coeffs[order, basis, 1] * col_coord
            for b in range(blocks):
                piece = slice(b * BLOCK, (b + 1) * BLOCK)
                spatial = row_part.reshape(kept // 8, 8, BLOCK) + col_part[None, :, piece]
                term = spatial.reshape(kept, BLOCK) * image[b * kept : (b + 1) * kept]
                matched[:, piece] = term if basis == 0 else matched[:, piece] + term
        shift = dithers[order]
        inside = (col_ids[0:1] >= shift) & (col_ids[0:1] < shift + (col_count - DITHER))
        weight = inv_var[0].astype(jnp.float32) * inside.astype(jnp.float32)
        num_ref[...] += pick(weight) * matched[...]
        if not edges:
            den_ref[...] += weight

    @pl.when(visit == visit_count - 1)
    def _():
        if edges:
            group = lax.axis_index("visit")
            width = outs[0].shape[1]
            for ahead, out_ref in enumerate(outs):
                at = pl.multiple_of(lax.rem(group + ahead, groups) * width, width)
                edge = num_ref[:, pl.ds(at, width)]
                whole = [edge[:INNER], inner[:, pl.ds(at, width)], edge[INNER:]]
                out_ref[...] = jnp.concatenate(whole, axis=0).astype(out_ref.dtype)
        else:
            inner_ref[...] = num_ref[...]
            split_strips(den_ref, outs)


def coadd_call(dithers, depths, coeffs, row_taps, col_taps, images, inv_var, halos, tiles, groups):
    visit_count, row_count, col_count = images.shape
    basis_count = row_taps.shape[0]
    edges = len(halos) > 0
    kept = 2 * INNER if edges else row_count - 2 * INNER
    width = col_count // groups
    slots = row_count + 2 * HALO if edges else row_count
    whole = lambda shape: pl.BlockSpec(shape, lambda v: (0,) * len(shape))
    scalar = pl.BlockSpec(memory_space=pltpu.SMEM)
    by_visit = lambda rows: pl.BlockSpec((1, rows, col_count), lambda v: (v, 0, 0))
    in_specs = [scalar] * 3 + [whole(row_taps.shape)] * 2 + [by_visit(row_count)] * 2
    shapes = [jax.ShapeDtypeStruct((row_count, width), jnp.float32)]
    shapes += [jax.ShapeDtypeStruct((row_count, width), jnp.bfloat16)] * (groups - 1)
    if edges:
        in_specs += [by_visit(halos[0].shape[1])] * 2 + [whole(halos[2].shape)]
        last = pltpu.VMEM((slots, col_count), jnp.bfloat16)
    else:
        shapes = [jax.ShapeDtypeStruct((kept, col_count), jnp.float32)] + shapes
        last = pltpu.VMEM((row_count, col_count), jnp.float32)
    streams = visit_count * basis_count * (kept * slots + kept * 2 * BLOCK) * 2 * col_count
    return pl.pallas_call(
        lambda *refs: coadd_kernel(
            *refs, total_rows=row_count * tiles, tiles=tiles, edges=edges, groups=groups
        ),
        out_shape=shapes,
        grid=(visit_count,),
        in_specs=in_specs,
        out_specs=[whole(shape.shape) for shape in shapes],
        scratch_shapes=[
            pltpu.VMEM((basis_count * kept, slots), jnp.bfloat16),
            pltpu.VMEM((basis_count, BLOCK + 2 * SIDE, BLOCK), jnp.bfloat16),
            pltpu.VMEM((2, 16, 512), jnp.float32),
            pltpu.VMEM((basis_count * kept, col_count + 2 * SIDE), jnp.bfloat16),
            pltpu.VMEM((kept, col_count), jnp.float32),
            pltpu.VMEM((kept, col_count), jnp.float32),
            last,
        ],
        compiler_params=pltpu.CompilerParams(
            dimension_semantics=("arbitrary",), vmem_limit_bytes=48 << 20
        ),
        cost_estimate=pl.CostEstimate(
            flops=streams, bytes_accessed=images.size * 4, transcendentals=0
        ),
        name="coadd_edges" if edges else "coadd_inner",
    )(dithers, depths, coeffs, row_taps, col_taps, images, inv_var, *halos)


def exchange(own, sends, axis):
    groups = len(sends) + 1
    for ahead in range(1, groups):
        got = lax.ppermute(
            sends[ahead - 1], axis, [(i, (i + ahead) % groups) for i in range(groups)]
        )
        own = own + got.astype(jnp.float32)
    return own


def local(images, inv_var, row_taps, col_taps, coeffs, dithers, depths):
    row_count = images.shape[1]
    tiles = lax.axis_size("sky")
    groups = lax.axis_size("visit")
    top = lax.ppermute(
        images[:, row_count - INNER :], "sky", [(i, i + 1) for i in range(tiles - 1)]
    )
    bottom = lax.ppermute(images[:, :INNER], "sky", [(i + 1, i) for i in range(tiles - 1)])
    given = (dithers, depths, coeffs, row_taps, col_taps, images, inv_var)
    inner, den_own, *den_sends = coadd_call(*given, (), tiles, groups)
    denominator = exchange(den_own, den_sends, "visit")
    num_own, *num_sends = coadd_call(*given, (top, bottom, inner), tiles, groups)
    numerator = exchange(num_own, num_sends, "visit")
    return numerator / (1.0 + denominator)


def solution(mesh):
    placed = (P("visit", "sky", None), P("visit", "sky", None), P(), P(), P(), P(), P("sky"))
    return jax.shard_map(
        local, mesh=mesh, in_specs=placed, out_specs=P("sky", "visit"), check_vma=False
    )
```

```python
import jax
import jax.numpy as jnp
from jax import lax
from jax.experimental import pallas as pl
from jax.experimental.pallas import tpu as pltpu
from jax.sharding import PartitionSpec as P

DITHER = 256
SIDE = 128
BLOCK = 256
HALO = 32
INNER = 24


def build_tables(row_taps, col_taps, rows_ref, cols_ref, laid, row_count):
    basis_count, tap_count = row_taps.shape
    half = tap_count // 2
    nothing = jnp.zeros((128, 128), jnp.bfloat16)
    tap = lax.broadcasted_iota(jnp.int32, (128, 512), 0)
    lane = lax.broadcasted_iota(jnp.int32, (128, 512), 1)
    for which, taps, target in (
        (0, row_taps, HALO - half + tap),
        (1, col_taps, SIDE + half - tap),
    ):
        laid[which] = jnp.zeros_like(laid[which])
        laid[which, 0:basis_count, 0:tap_count] = taps[...].astype(jnp.float32)
        picks = ((lane == target) & (tap < tap_count)).astype(jnp.bfloat16)
        laid[which] = jnp.dot(
            laid[which, :, 0:128].astype(jnp.bfloat16), picks, preferred_element_type=jnp.float32
        )

    def step(basis, carry):
        wide = jnp.broadcast_to(laid[0, pl.ds(basis, 1), 0:256], (row_count, 256))
        wide = pltpu.roll(wide, 0, 1, stride=1, stride_axis=0).astype(jnp.bfloat16)
        at = pl.multiple_of(basis * row_count, row_count)
        rows_ref[pl.ds(at, row_count), :] = wide[:, : rows_ref.shape[1]]
        band = jnp.broadcast_to(laid[1, pl.ds(basis, 1), :], (128, 512))
        band = pltpu.roll(band, 0, 1, stride=1, stride_axis=0).astype(jnp.bfloat16)
        for p in range(cols_ref.shape[1] // 128):
            for x in range(cols_ref.shape[2] // 128):
                apart = p - x
                piece = band[:, (2 - apart) * 128 : (3 - apart) * 128] if 0 <= apart < 3 else nothing
                cols_ref[basis, p * 128 : (p + 1) * 128, x * 128 : (x + 1) * 128] = piece
        return carry

    lax.fori_loop(0, basis_count, step, 0)


def split_strips(sums, out_refs):
    groups = len(out_refs)
    width = out_refs[0].shape[2]
    group = lax.axis_index("visit")
    for ahead, out_ref in enumerate(out_refs):
        at = pl.multiple_of(lax.rem(group + ahead, groups) * width, width)
        for which, total in enumerate(sums):
            out_ref[which] = total[:, pl.ds(at, width)].astype(out_ref.dtype)


def coadd_kernel(
    dithers, depths, coeffs, row_taps, col_taps, images, inv_var, top, bottom, *rest,
    total_rows, tiles, first_visit, visit_count,
):
    opening = first_visit == 0
    earlier, outs = ((), rest[:-8]) if opening else (rest[:2], rest[2:-8])
    rows_ref, cols_ref, laid, passed, matched, source, num_ref, den_ref = rest[-8:]
    step = pl.program_id(0)
    steps = pl.num_programs(0)
    row_count, col_count = images.shape[1:]
    basis_count = row_taps.shape[0]
    blocks = col_count // BLOCK
    visits_all = dithers.shape[0]
    sky = lax.axis_index("sky")
    order = lax.axis_index("visit") * visit_count + first_visit + step

    def is_covered(order):
        return lax.rem(order - sky * visits_all // tiles + visits_all, visits_all) < depths[0]

    def weight_of(order, values):
        col_ids = lax.broadcasted_iota(jnp.int32, (1, col_count), 1)
        shift = dithers[order]
        inside = (col_ids >= shift) & (col_ids < shift + (col_count - DITHER))
        return values.astype(jnp.float32) * inside.astype(jnp.float32)

    @pl.when(step == 0)
    def _():
        passed[:, 0:SIDE] = jnp.zeros((passed.shape[0], SIDE), jnp.bfloat16)
        passed[:, SIDE + col_count :] = jnp.zeros((passed.shape[0], SIDE), jnp.bfloat16)
        source[...] = jnp.zeros_like(source)
        build_tables(row_taps, col_taps, rows_ref, cols_ref, laid, row_count)
        if opening:
            num_ref[...] = jnp.zeros_like(num_ref)
            den_ref[...] = jnp.zeros_like(den_ref)
        else:
            num_ref[...] = earlier[0][...]
            den_ref[...] = earlier[1][...]

    @pl.when(is_covered(order))
    def _():
        half = top.shape[1]
        source[HALO - half : HALO, :] = top[0]
        source[HALO : HALO + row_count, :] = images[0]
        source[HALO + row_count : HALO + row_count + half, :] = bottom[0]
        for b in range(blocks):
            piece = slice(b * BLOCK, (b + 1) * BLOCK)
            out = jnp.dot(rows_ref[...], source[:, piece], preferred_element_type=jnp.float32)
            passed[:, SIDE + b * BLOCK : SIDE + (b + 1) * BLOCK] = out.astype(jnp.bfloat16)
        row_ids = sky * row_count + lax.broadcasted_iota(jnp.int32, (row_count, 128), 0)
        row_coord = (2.0 * row_ids.astype(jnp.float32) + 1.0) / total_rows - 1.0
        col_ids = lax.broadcasted_iota(jnp.int32, (8, col_count), 1)
        col_coord = (2.0 * col_ids.astype(jnp.float32) + 1.0) / col_count - 1.0
        for basis in range(basis_count):
            band = slice(basis * row_count, (basis + 1) * row_count)
            lhs = jnp.concatenate(
                [passed[band, b * BLOCK : (b + 2) * BLOCK] for b in range(blocks)], axis=0
            )
            image = jnp.dot(lhs, cols_ref[basis], preferred_element_type=jnp.float32)
            row_part = coeffs[order, basis, 0] + coeffs[order, basis, 2] * row_coord
            row_part = jnp.concatenate([row_part, row_part], axis=1)
            col_part = coeffs[order, basis, 1] * col_coord
            for b in range(blocks):
                piece = slice(b * BLOCK, (b + 1) * BLOCK)
                spatial = row_part.reshape(row_count // 8, 8, BLOCK) + col_part[None, :, piece]
                term = spatial.reshape(row_count, BLOCK) * image[b * row_count : (b + 1) * row_count]
                matched[:, piece] = term if basis == 0 else matched[:, piece] + term
        weight = weight_of(order, inv_var[0])
        num_ref[...] += weight * matched[...]
        den_ref[...] += weight

    @pl.when(step == steps - 1)
    def _():
        if opening:
            outs[0][...] = num_ref[...]
            outs[1][...] = den_ref[...]
        else:
            split_strips((num_ref, den_ref), outs)


def coadd_call(given, top, bottom, earlier, first_visit, tiles, groups):
    *small, images, inv_var = given
    visit_count, row_count, col_count = images.shape
    basis_count = small[3].shape[0]
    opening = first_visit == 0
    steps = top.shape[0]
    width = col_count // groups
    slots = row_count + 2 * HALO
    plane = (row_count, col_count)
    whole = lambda shape: pl.BlockSpec(shape, lambda v: (0,) * len(shape))
    by_visit = lambda rows, at: pl.BlockSpec((1, rows, col_count), lambda v: (v + at, 0, 0))
    in_specs = [pl.BlockSpec(memory_space=pltpu.SMEM)] * 3 + [whole(small[3].shape)] * 2
    in_specs += [by_visit(row_count, first_visit)] * 2 + [by_visit(top.shape[1], 0)] * 2
    in_specs += [whole(plane)] * len(earlier)
    if opening:
        shapes = [jax.ShapeDtypeStruct(plane, jnp.float32)] * 2
    else:
        shapes = [jax.ShapeDtypeStruct((2, row_count, width), jnp.float32)]
        shapes += [jax.ShapeDtypeStruct((2, row_count, width), jnp.bfloat16)] * (groups - 1)
    flops = steps * basis_count * row_count * (slots + 2 * BLOCK) * 2 * col_count
    return pl.pallas_call(
        lambda *refs: coadd_kernel(
            *refs,
            total_rows=row_count * tiles,
            tiles=tiles,
            first_visit=first_visit,
            visit_count=visit_count,
        ),
        out_shape=shapes,
        grid=(steps,),
        in_specs=in_specs,
        out_specs=[whole(shape.shape) for shape in shapes],
        scratch_shapes=[
            pltpu.VMEM((basis_count * row_count, slots), jnp.bfloat16),
            pltpu.VMEM((basis_count, BLOCK + 2 * SIDE, BLOCK), jnp.bfloat16),
            pltpu.VMEM((2, 16, 512), jnp.float32),
            pltpu.VMEM((basis_count * row_count, col_count + 2 * SIDE), jnp.bfloat16),
            pltpu.VMEM(plane, jnp.float32),
            pltpu.VMEM((slots, col_count), jnp.bfloat16),
        ]
        + [pltpu.VMEM(plane, jnp.float32)] * 2,
        compiler_params=pltpu.CompilerParams(
            dimension_semantics=("arbitrary",), vmem_limit_bytes=48 << 20
        ),
        cost_estimate=pl.CostEstimate(
            flops=flops, bytes_accessed=images.size * 2, transcendentals=0
        ),
        name="coadd_opening" if opening else "coadd_closing",
    )(*small, images, inv_var, top, bottom, *earlier)


def exchange(own, sends, axis):
    groups = len(sends) + 1
    for ahead in range(1, groups):
        got = lax.ppermute(
            sends[ahead - 1], axis, [(i, (i + ahead) % groups) for i in range(groups)]
        )
        own = own + got.astype(jnp.float32)
    return own


def halos(images, rows):
    tiles = lax.axis_size("sky")
    top = lax.ppermute(
        images[:, images.shape[1] - rows :], "sky", [(i, i + 1) for i in range(tiles - 1)]
    )
    bottom = lax.ppermute(images[:, :rows], "sky", [(i + 1, i) for i in range(tiles - 1)])
    return top, bottom


def local(images, inv_var, row_taps, col_taps, coeffs, dithers, depths):
    tiles = lax.axis_size("sky")
    groups = lax.axis_size("visit")
    half = images.shape[0] // 2
    near = halos(images[:half], INNER)
    far = halos(images[half:], INNER)
    given = (dithers, depths, coeffs, row_taps, col_taps, images, inv_var)
    earlier = coadd_call(given, *near, (), 0, tiles, groups)
    own, *sends = coadd_call(given, *far, earlier, half, tiles, groups)
    numerator, denominator = exchange(own, sends, "visit")
    return numerator / (1.0 + denominator)


def solution(mesh):
    placed = (P("visit", "sky", None), P("visit", "sky", None), P(), P(), P(), P(), P("sky"))
    return jax.shard_map(
        local, mesh=mesh, in_specs=placed, out_specs=P("sky", "visit"), check_vma=False
    )
```

```python
import jax
import jax.numpy as jnp
from jax import lax
from jax.experimental import pallas as pl
from jax.experimental.pallas import tpu as pltpu
from jax.sharding import PartitionSpec as P

DITHER = 256
SIDE = 128
BLOCK = 256
HALO = 32
INNER = 24


def build_tables(row_taps, col_taps, rows_ref, cols_ref, laid, row_count, above, runs):
    basis_count, tap_count = row_taps.shape
    half = tap_count // 2
    kept = rows_ref.shape[0] // basis_count
    nothing = jnp.zeros((128, 128), jnp.bfloat16)
    tap = lax.broadcasted_iota(jnp.int32, (128, 512), 0)
    lane = lax.broadcasted_iota(jnp.int32, (128, 512), 1)
    for which, taps, target in (
        (0, row_taps, lax.rem(above - half + tap + 256, 256)),
        (1, col_taps, SIDE + half - tap),
    ):
        laid[which] = jnp.zeros_like(laid[which])
        laid[which, 0:basis_count, 0:tap_count] = taps[...].astype(jnp.float32)
        picks = ((lane == target) & (tap < tap_count)).astype(jnp.bfloat16)
        laid[which] = jnp.dot(
            laid[which, :, 0:128].astype(jnp.bfloat16), picks, preferred_element_type=jnp.float32
        )

    def step(basis, carry):
        wide = jnp.broadcast_to(laid[0, pl.ds(basis, 1), 0:256], (row_count, 256))
        wide = pltpu.roll(wide, 0, 1, stride=1, stride_axis=0)
        wide = jnp.concatenate([wide[first:last] for first, last in runs], axis=0)
        at = pl.multiple_of(basis * kept, kept)
        rows_ref[pl.ds(at, kept), :] = wide[:, : rows_ref.shape[1]].astype(jnp.bfloat16)
        band = jnp.broadcast_to(laid[1, pl.ds(basis, 1), :], (128, 512))
        band = pltpu.roll(band, 0, 1, stride=1, stride_axis=0).astype(jnp.bfloat16)
        for p in range(cols_ref.shape[1] // 128):
            for x in range(cols_ref.shape[2] // 128):
                apart = p - x
                piece = band[:, (2 - apart) * 128 : (3 - apart) * 128] if 0 <= apart < 3 else nothing
                cols_ref[basis, p * 128 : (p + 1) * 128, x * 128 : (x + 1) * 128] = piece
        return carry

    lax.fori_loop(0, basis_count, step, 0)


def split_strips(total, out_refs):
    groups = len(out_refs)
    width = out_refs[0].shape[1]
    group = lax.axis_index("visit")
    for ahead, out_ref in enumerate(out_refs):
        at = pl.multiple_of(lax.rem(group + ahead, groups) * width, width)
        out_ref[...] = total[:, pl.ds(at, width)].astype(out_ref.dtype)


def coadd_kernel(dithers, depths, coeffs, row_taps, col_taps, images, inv_var, *rest, total_rows, tiles, edges, groups):
    visit = pl.program_id(0)
    visit_count = pl.num_programs(0)
    row_count, col_count = images.shape[1:]
    basis_count = row_taps.shape[0]
    blocks = col_count // BLOCK
    visits_all = dithers.shape[0]
    sky = lax.axis_index("sky")
    order = lax.axis_index("visit") * visit_count + visit
    covered = lax.rem(order - sky * visits_all // tiles + visits_all, visits_all) < depths[0]
    if edges:
        top, bottom, inner = rest[:3]
        outs, (rows_ref, cols_ref, laid, passed, matched, num_ref, source) = (
            rest[3 : 3 + groups],
            rest[3 + groups :],
        )
        runs = ((0, INNER), (row_count - INNER, row_count))
        above = HALO
    else:
        inner_ref = rest[0]
        outs, (rows_ref, cols_ref, laid, passed, matched, num_ref, den_ref) = (
            rest[1 : 1 + groups],
            rest[1 + groups :],
        )
        runs = ((INNER, row_count - INNER),)
        above = 0
    kept = sum(last - first for first, last in runs)

    def pick(value):
        return jnp.concatenate([value[first:last] for first, last in runs], axis=0)

    @pl.when(visit == 0)
    def _():
        passed[:, 0:SIDE] = jnp.zeros((passed.shape[0], SIDE), jnp.bfloat16)
        passed[:, SIDE + col_count :] = jnp.zeros((passed.shape[0], SIDE), jnp.bfloat16)
        build_tables(row_taps, col_taps, rows_ref, cols_ref, laid, row_count, above, runs)
        num_ref[...] = jnp.zeros_like(num_ref)
        if edges:
            source[...] = jnp.zeros_like(source)
        else:
            den_ref[...] = jnp.zeros_like(den_ref)

    @pl.when(covered)
    def _():
        if edges:
            half = top.shape[1]
            source[HALO - half : HALO, :] = top[visit]
            source[HALO : HALO + row_count, :] = images[0]
            source[HALO + row_count : HALO + row_count + half, :] = bottom[visit]
        for b in range(blocks):
            piece = slice(b * BLOCK, (b + 1) * BLOCK)
            data = source[:, piece] if edges else images[0, :, piece]
            out = jnp.dot(rows_ref[...], data, preferred_element_type=jnp.float32)
            passed[:, SIDE + b * BLOCK : SIDE + (b + 1) * BLOCK] = out.astype(jnp.bfloat16)
        row_ids = sky * row_count + lax.broadcasted_iota(jnp.int32, (row_count, 128), 0)
        row_coord = pick((2.0 * row_ids.astype(jnp.float32) + 1.0) / total_rows - 1.0)
        col_ids = lax.broadcasted_iota(jnp.int32, (8, col_count), 1)
        col_coord = (2.0 * col_ids.astype(jnp.float32) + 1.0) / col_count - 1.0
        for basis in range(basis_count):
            band = slice(basis * kept, (basis + 1) * kept)
            lhs = jnp.concatenate(
                [passed[band, b * BLOCK : (b + 2) * BLOCK] for b in range(blocks)], axis=0
            )
            image = jnp.dot(lhs, cols_ref[basis], preferred_element_type=jnp.float32)
            row_part = coeffs[basis, 0, order] + coeffs[basis, 2, order] * row_coord
            row_part = jnp.concatenate([row_part, row_part], axis=1)
            col_part = coeffs[basis, 1, order] * col_coord
            for b in range(blocks):
                piece = slice(b * BLOCK, (b + 1) * BLOCK)
                spatial = row_part.reshape(kept // 8, 8, BLOCK) + col_part[None, :, piece]
                term = spatial.reshape(kept, BLOCK) * image[b * kept : (b + 1) * kept]
                matched[:, piece] = term if basis == 0 else matched[:, piece] + term
        shift = dithers[order]
        inside = (col_ids[0:1] >= shift) & (col_ids[0:1] < shift + (col_count - DITHER))
        weight = inv_var[0].astype(jnp.float32) * inside.astype(jnp.float32)
        num_ref[...] += pick(weight) * matched[...]
        if not edges:
            den_ref[...] += weight

    @pl.when(visit == visit_count - 1)
    def _():
        if edges:
            group = lax.axis_index("visit")
            width = outs[0].shape[1]
            for ahead, out_ref in enumerate(outs):
                at = pl.multiple_of(lax.rem(group + ahead, groups) * width, width)
                edge = num_ref[:, pl.ds(at, width)]
                whole = [edge[:INNER], inner[:, pl.ds(at, width)], edge[INNER:]]
                out_ref[...] = jnp.concatenate(whole, axis=0).astype(out_ref.dtype)
        else:
            inner_ref[...] = num_ref[...]
            split_strips(den_ref, outs)


def coadd_call(dithers, depths, coeffs, row_taps, col_taps, images, inv_var, halos, tiles, groups):
    visit_count, row_count, col_count = images.shape
    basis_count = row_taps.shape[0]
    edges = len(halos) > 0
    kept = 2 * INNER if edges else row_count - 2 * INNER
    width = col_count // groups
    slots = row_count + 2 * HALO if edges else row_count
    whole = lambda shape: pl.BlockSpec(shape, lambda v: (0,) * len(shape))
    scalar = pl.BlockSpec(memory_space=pltpu.SMEM)
    by_visit = lambda rows: pl.BlockSpec((1, rows, col_count), lambda v: (v, 0, 0))
    in_specs = [scalar] * 3 + [whole(row_taps.shape)] * 2 + [by_visit(row_count)] * 2
    shapes = [jax.ShapeDtypeStruct((row_count, width), jnp.float32)]
    shapes += [jax.ShapeDtypeStruct((row_count, width), jnp.bfloat16)] * (groups - 1)
    if edges:
        in_specs += [pl.BlockSpec(memory_space=pltpu.VMEM)] * 2 + [whole(halos[2].shape)]
        last = pltpu.VMEM((slots, col_count), jnp.bfloat16)
    else:
        shapes = [jax.ShapeDtypeStruct((kept, col_count), jnp.float32)] + shapes
        last = pltpu.VMEM((row_count, col_count), jnp.float32)
    streams = visit_count * basis_count * (kept * slots + kept * 2 * BLOCK) * 2 * col_count
    return pl.pallas_call(
        lambda *refs: coadd_kernel(
            *refs, total_rows=row_count * tiles, tiles=tiles, edges=edges, groups=groups
        ),
        out_shape=shapes,
        grid=(visit_count,),
        in_specs=in_specs,
        out_specs=[whole(shape.shape) for shape in shapes],
        scratch_shapes=[
            pltpu.VMEM((basis_count * kept, slots), jnp.bfloat16),
            pltpu.VMEM((basis_count, BLOCK + 2 * SIDE, BLOCK), jnp.bfloat16),
            pltpu.VMEM((2, 16, 512), jnp.float32),
            pltpu.VMEM((basis_count * kept, col_count + 2 * SIDE), jnp.bfloat16),
            pltpu.VMEM((kept, col_count), jnp.float32),
            pltpu.VMEM((kept, col_count), jnp.float32),
            last,
        ],
        compiler_params=pltpu.CompilerParams(
            dimension_semantics=("arbitrary",), vmem_limit_bytes=(50 if edges else 61) << 20
        ),
        cost_estimate=pl.CostEstimate(
            flops=streams, bytes_accessed=images.size * 4, transcendentals=0
        ),
        name="coadd_edges" if edges else "coadd_inner",
    )(dithers, depths, coeffs, row_taps, col_taps, images, inv_var, *halos)


def exchange(own, sends, axis):
    groups = len(sends) + 1
    for ahead in range(1, groups):
        got = lax.ppermute(
            sends[ahead - 1], axis, [(i, (i + ahead) % groups) for i in range(groups)]
        )
        own = own + got.astype(jnp.float32)
    return own


def local(images, inv_var, row_taps, col_taps, coeffs, dithers, depths):
    row_count = images.shape[1]
    tiles = lax.axis_size("sky")
    groups = lax.axis_size("visit")
    top = lax.ppermute(
        images[:, row_count - INNER :], "sky", [(i, i + 1) for i in range(tiles - 1)]
    )
    bottom = lax.ppermute(images[:, :INNER], "sky", [(i + 1, i) for i in range(tiles - 1)])
    given = (dithers, depths, coeffs.transpose(1, 2, 0), row_taps, col_taps, images, inv_var)
    inner, den_own, *den_sends = coadd_call(*given, (), tiles, groups)
    denominator = exchange(den_own, den_sends, "visit")
    num_own, *num_sends = coadd_call(*given, (top, bottom, inner), tiles, groups)
    numerator = exchange(num_own, num_sends, "visit")
    return numerator / (1.0 + denominator)


def solution(mesh):
    placed = (P("visit", "sky", None), P("visit", "sky", None), P(), P(), P(), P(), P("sky"))
    return jax.shard_map(
        local, mesh=mesh, in_specs=placed, out_specs=P("sky", "visit"), check_vma=False
    )
```

```python
import jax
import jax.numpy as jnp
from jax import lax
from jax.experimental import pallas as pl
from jax.experimental.pallas import tpu as pltpu
from jax.sharding import PartitionSpec as P

DITHER = 256
SIDE = 128
BLOCK = 256
HALO = 32
INNER = 24
STRIDE = 216


def build_tables(row_taps, col_taps, rows_ref, cols_ref, laid, row_count, above, runs):
    basis_count, tap_count = row_taps.shape
    half = tap_count // 2
    kept = rows_ref.shape[0] // basis_count
    tap = lax.broadcasted_iota(jnp.int32, (128, 512), 0)
    lane = lax.broadcasted_iota(jnp.int32, (128, 512), 1)
    for which, taps, target in (
        (0, row_taps, lax.rem(above - half + tap + 256, 256)),
        (1, col_taps, 256 - tap),
    ):
        laid[which] = jnp.zeros_like(laid[which])
        laid[which, 0:basis_count, 0:tap_count] = taps[...].astype(jnp.float32)
        picks = ((lane == target) & (tap < tap_count)).astype(jnp.bfloat16)
        laid[which] = jnp.dot(
            laid[which, :, 0:128].astype(jnp.bfloat16), picks, preferred_element_type=jnp.float32
        )

    def step(basis, carry):
        wide = jnp.broadcast_to(laid[0, pl.ds(basis, 1), 0:256], (row_count, 256))
        wide = pltpu.roll(wide, 0, 1, stride=1, stride_axis=0)
        wide = jnp.concatenate([wide[first:last] for first, last in runs], axis=0)
        at = pl.multiple_of(basis * kept, kept)
        rows_ref[pl.ds(at, kept), :] = wide[:, : rows_ref.shape[1]].astype(jnp.bfloat16)
        band = jnp.broadcast_to(laid[1, pl.ds(basis, 1), :], (256, 512))
        band = pltpu.roll(band, 0, 1, stride=1, stride_axis=0).astype(jnp.bfloat16)
        cols_ref[basis] = band[:, 256:512]
        return carry

    lax.fori_loop(0, basis_count, step, 0)


def split_strips(total, out_refs):
    groups = len(out_refs)
    width = out_refs[0].shape[1]
    group = lax.axis_index("visit")
    for ahead, out_ref in enumerate(out_refs):
        at = pl.multiple_of(lax.rem(group + ahead, groups) * width, width)
        out_ref[...] = total[:, pl.ds(at, width)].astype(out_ref.dtype)


def coadd_kernel(dithers, depths, coeffs, row_taps, col_taps, images, inv_var, *rest, total_rows, tiles, edges, groups):
    visit = pl.program_id(0)
    visit_count = pl.num_programs(0)
    row_count, col_count = images.shape[1:]
    basis_count = row_taps.shape[0]
    blocks = -(-col_count // STRIDE)
    reach = row_taps.shape[1] // 2
    visits_all = dithers.shape[0]
    sky = lax.axis_index("sky")
    order = lax.axis_index("visit") * visit_count + visit
    covered = lax.rem(order - sky * visits_all // tiles + visits_all, visits_all) < depths[0]
    if edges:
        top, bottom, inner = rest[:3]
        outs, (rows_ref, cols_ref, laid, passed, matched, num_ref, source, plain) = (
            rest[3 : 3 + groups],
            rest[3 + groups :],
        )
        runs = ((0, INNER), (row_count - INNER, row_count))
        above = HALO
    else:
        inner_ref = rest[0]
        outs, (rows_ref, cols_ref, laid, passed, matched, num_ref, source, den_ref) = (
            rest[1 : 1 + groups],
            rest[1 + groups :],
        )
        runs = ((INNER, row_count - INNER),)
        above = 0
    kept = sum(last - first for first, last in runs)

    def pick(value):
        return jnp.concatenate([value[first:last] for first, last in runs], axis=0)

    @pl.when(visit == 0)
    def _():
        build_tables(row_taps, col_taps, rows_ref, cols_ref, laid, row_count, above, runs)
        num_ref[...] = jnp.zeros_like(num_ref)
        source[...] = jnp.zeros_like(source)
        if not edges:
            den_ref[...] = jnp.zeros_like(den_ref)

    @pl.when(covered)
    def _():
        middle = slice(SIDE, SIDE + col_count)
        source[above : above + row_count, middle] = images[0]
        if edges:
            half = top.shape[1]
            source[HALO - half : HALO, middle] = top[visit]
            source[HALO + row_count : HALO + row_count + half, middle] = bottom[visit]
        for b in range(blocks):
            piece = slice(b * BLOCK, (b + 1) * BLOCK)
            begin = SIDE - reach + b * STRIDE
            tile = begin // 128 * 128
            data = source[:, tile : tile + 384][:, begin - tile : begin - tile + BLOCK]
            out = jnp.dot(rows_ref[...], data, preferred_element_type=jnp.float32)
            passed[:, piece] = out.astype(jnp.bfloat16)
        row_ids = sky * row_count + lax.broadcasted_iota(jnp.int32, (row_count, 128), 0)
        row_coord = pick((2.0 * row_ids.astype(jnp.float32) + 1.0) / total_rows - 1.0)
        lanes = lax.broadcasted_iota(jnp.int32, (8, BLOCK), 1)
        col_ids = jnp.concatenate([lanes + b * STRIDE for b in range(blocks)], axis=1)
        col_coord = (2.0 * col_ids.astype(jnp.float32) + 1.0) / col_count - 1.0
        for basis in range(basis_count):
            band = slice(basis * kept, (basis + 1) * kept)
            lhs = jnp.concatenate(
                [passed[band, b * BLOCK : (b + 1) * BLOCK] for b in range(blocks)], axis=0
            )
            image = jnp.dot(lhs, cols_ref[basis], preferred_element_type=jnp.float32)
            row_part = coeffs[basis, 0, order] + coeffs[basis, 2, order] * row_coord
            row_part = jnp.concatenate([row_part, row_part], axis=1)
            col_part = coeffs[basis, 1, order] * col_coord
            for b in range(blocks):
                piece = slice(b * BLOCK, (b + 1) * BLOCK)
                spatial = row_part.reshape(kept // 8, 8, BLOCK) + col_part[None, :, piece]
                term = spatial.reshape(kept, BLOCK) * image[b * kept : (b + 1) * kept]
                matched[:, piece] = term if basis == 0 else matched[:, piece] + term
        shift = dithers[order]
        values = inv_var[0].astype(jnp.float32)
        chosen = pick(values)
        for b in range(blocks):
            piece = slice(b * BLOCK, (b + 1) * BLOCK)
            ids = col_ids[0:1, piece]
            inside = (ids >= shift) & (ids < shift + (col_count - DITHER))
            begin = b * STRIDE
            part = chosen[:, begin : min(begin + BLOCK, col_count)]
            if part.shape[1] < BLOCK:
                part = jnp.concatenate([part, jnp.zeros((kept, BLOCK - part.shape[1]), jnp.float32)], axis=1)
            num_ref[:, piece] += part * inside.astype(jnp.float32) * matched[:, piece]
        if not edges:
            ids = lax.broadcasted_iota(jnp.int32, (1, col_count), 1)
            inside = (ids >= shift) & (ids < shift + (col_count - DITHER))
            den_ref[...] += values * inside.astype(jnp.float32)

    def unwindowed():
        parts = [
            num_ref[:, b * BLOCK : b * BLOCK + BLOCK][:, : min(STRIDE, col_count - b * STRIDE)]
            for b in range(blocks)
        ]
        return jnp.concatenate(parts, axis=1)

    @pl.when(visit == visit_count - 1)
    def _():
        if edges:
            plain[...] = unwindowed()
            group = lax.axis_index("visit")
            width = outs[0].shape[1]
            for ahead, out_ref in enumerate(outs):
                at = pl.multiple_of(lax.rem(group + ahead, groups) * width, width)
                edge = plain[:, pl.ds(at, width)]
                whole = [edge[:INNER], inner[:, pl.ds(at, width)], edge[INNER:]]
                out_ref[...] = jnp.concatenate(whole, axis=0).astype(out_ref.dtype)
        else:
            inner_ref[...] = unwindowed()
            split_strips(den_ref, outs)


def coadd_call(dithers, depths, coeffs, row_taps, col_taps, images, inv_var, halos, tiles, groups):
    visit_count, row_count, col_count = images.shape
    basis_count = row_taps.shape[0]
    edges = len(halos) > 0
    kept = 2 * INNER if edges else row_count - 2 * INNER
    width = col_count // groups
    windows = -(-col_count // STRIDE)
    slots = row_count + 2 * HALO if edges else row_count
    whole = lambda shape: pl.BlockSpec(shape, lambda v: (0,) * len(shape))
    scalar = pl.BlockSpec(memory_space=pltpu.SMEM)
    by_visit = lambda rows: pl.BlockSpec((1, rows, col_count), lambda v: (v, 0, 0))
    in_specs = [scalar] * 3 + [whole(row_taps.shape)] * 2 + [by_visit(row_count)] * 2
    shapes = [jax.ShapeDtypeStruct((row_count, width), jnp.float32)]
    shapes += [jax.ShapeDtypeStruct((row_count, width), jnp.bfloat16)] * (groups - 1)
    if edges:
        in_specs += [pl.BlockSpec(memory_space=pltpu.VMEM)] * 2 + [whole(halos[2].shape)]
        last = pltpu.VMEM((kept, col_count), jnp.float32)
    else:
        shapes = [jax.ShapeDtypeStruct((kept, col_count), jnp.float32)] + shapes
        last = pltpu.VMEM((row_count, col_count), jnp.float32)
    streams = visit_count * basis_count * (kept * slots + kept * BLOCK) * 2 * col_count
    return pl.pallas_call(
        lambda *refs: coadd_kernel(
            *refs, total_rows=row_count * tiles, tiles=tiles, edges=edges, groups=groups
        ),
        out_shape=shapes,
        grid=(visit_count,),
        in_specs=in_specs,
        out_specs=[whole(shape.shape) for shape in shapes],
        scratch_shapes=[
            pltpu.VMEM((basis_count * kept, slots), jnp.bfloat16),
            pltpu.VMEM((basis_count, BLOCK, BLOCK), jnp.bfloat16),
            pltpu.VMEM((2, 16, 512), jnp.float32),
            pltpu.VMEM((basis_count * kept, windows * BLOCK), jnp.bfloat16),
            pltpu.VMEM((kept, windows * BLOCK), jnp.float32),
            pltpu.VMEM((kept, windows * BLOCK), jnp.float32),
            pltpu.VMEM((slots, col_count + 4 * SIDE), jnp.bfloat16),
            last,
        ],
        compiler_params=pltpu.CompilerParams(
            dimension_semantics=("arbitrary",), vmem_limit_bytes=(50 if edges else 61) << 20
        ),
        cost_estimate=pl.CostEstimate(
            flops=streams, bytes_accessed=images.size * 4, transcendentals=0
        ),
        name="coadd_edges" if edges else "coadd_inner",
    )(dithers, depths, coeffs, row_taps, col_taps, images, inv_var, *halos)


def exchange(own, sends, axis):
    groups = len(sends) + 1
    for ahead in range(1, groups):
        got = lax.ppermute(
            sends[ahead - 1], axis, [(i, (i + ahead) % groups) for i in range(groups)]
        )
        own = own + got.astype(jnp.float32)
    return own


def local(images, inv_var, row_taps, col_taps, coeffs, dithers, depths):
    row_count = images.shape[1]
    tiles = lax.axis_size("sky")
    groups = lax.axis_size("visit")
    top = lax.ppermute(
        images[:, row_count - INNER :], "sky", [(i, i + 1) for i in range(tiles - 1)]
    )
    bottom = lax.ppermute(images[:, :INNER], "sky", [(i + 1, i) for i in range(tiles - 1)])
    given = (dithers, depths, coeffs.transpose(1, 2, 0), row_taps, col_taps, images, inv_var)
    inner, den_own, *den_sends = coadd_call(*given, (), tiles, groups)
    denominator = exchange(den_own, den_sends, "visit")
    num_own, *num_sends = coadd_call(*given, (top, bottom, inner), tiles, groups)
    numerator = exchange(num_own, num_sends, "visit")
    return numerator / (1.0 + denominator)


def solution(mesh):
    placed = (P("visit", "sky", None), P("visit", "sky", None), P(), P(), P(), P(), P("sky"))
    return jax.shard_map(
        local, mesh=mesh, in_specs=placed, out_specs=P("sky", "visit"), check_vma=False
    )
```

```python
import jax
import jax.numpy as jnp
from jax import lax
from jax.experimental import pallas as pl
from jax.experimental.pallas import tpu as pltpu
from jax.sharding import PartitionSpec as P

DITHER = 256
SIDE = 128
BLOCK = 256
HALO = 32
INNER = 24


def build_tables(row_taps, col_taps, rows_ref, cols_ref, laid, row_count, above, runs):
    basis_count, tap_count = row_taps.shape
    half = tap_count // 2
    kept = rows_ref.shape[0] // basis_count
    nothing = jnp.zeros((128, 128), jnp.bfloat16)
    tap = lax.broadcasted_iota(jnp.int32, (128, 512), 0)
    lane = lax.broadcasted_iota(jnp.int32, (128, 512), 1)
    for which, taps, target in (
        (0, row_taps, lax.rem(above - half + tap + 256, 256)),
        (1, col_taps, SIDE + half - tap),
    ):
        laid[which] = jnp.zeros_like(laid[which])
        laid[which, 0:basis_count, 0:tap_count] = taps[...].astype(jnp.float32)
        picks = ((lane == target) & (tap < tap_count)).astype(jnp.bfloat16)
        laid[which] = jnp.dot(
            laid[which, :, 0:128].astype(jnp.bfloat16), picks, preferred_element_type=jnp.float32
        )

    def step(basis, carry):
        wide = jnp.broadcast_to(laid[0, pl.ds(basis, 1), 0:256], (row_count, 256))
        wide = pltpu.roll(wide, 0, 1, stride=1, stride_axis=0)
        wide = jnp.concatenate([wide[first:last] for first, last in runs], axis=0)
        at = pl.multiple_of(basis * kept, kept)
        rows_ref[pl.ds(at, kept), :] = wide[:, : rows_ref.shape[1]].astype(jnp.bfloat16)
        band = jnp.broadcast_to(laid[1, pl.ds(basis, 1), :], (128, 512))
        band = pltpu.roll(band, 0, 1, stride=1, stride_axis=0).astype(jnp.bfloat16)
        for p in range(cols_ref.shape[1] // 128):
            for x in range(cols_ref.shape[2] // 128):
                apart = p - x
                piece = band[:, (2 - apart) * 128 : (3 - apart) * 128] if 0 <= apart < 3 else nothing
                cols_ref[basis, p * 128 : (p + 1) * 128, x * 128 : (x + 1) * 128] = piece
        return carry

    lax.fori_loop(0, basis_count, step, 0)


def split_strips(total, out_refs):
    groups = len(out_refs)
    width = out_refs[0].shape[1]
    group = lax.axis_index("visit")
    for ahead, out_ref in enumerate(out_refs):
        at = pl.multiple_of(lax.rem(group + ahead, groups) * width, width)
        out_ref[...] = total[:, pl.ds(at, width)].astype(out_ref.dtype)


def coadd_kernel(dithers, depths, coeffs, row_taps, col_taps, images, inv_var, *rest, total_rows, tiles, edges, groups):
    visit = pl.program_id(0)
    visit_count = pl.num_programs(0)
    row_count, col_count = images.shape[1:]
    basis_count = row_taps.shape[0]
    blocks = col_count // BLOCK
    visits_all = dithers.shape[0]
    sky = lax.axis_index("sky")
    order = lax.axis_index("visit") * visit_count + visit
    covered = lax.rem(order - sky * visits_all // tiles + visits_all, visits_all) < depths[0]
    if edges:
        top, bottom, inner = rest[:3]
        outs, (rows_ref, cols_ref, laid, passed, matched, num_ref, source) = (
            rest[3 : 3 + groups],
            rest[3 + groups :],
        )
        runs = ((0, INNER), (row_count - INNER, row_count))
        above = HALO
    else:
        inner_ref = rest[0]
        outs, (rows_ref, cols_ref, laid, passed, matched, num_ref, den_ref) = (
            rest[1 : 1 + groups],
            rest[1 + groups :],
        )
        runs = ((INNER, row_count - INNER),)
        above = 0
    kept = sum(last - first for first, last in runs)

    def pick(value):
        return jnp.concatenate([value[first:last] for first, last in runs], axis=0)

    @pl.when(visit == 0)
    def _():
        passed[:, 0:SIDE] = jnp.zeros((passed.shape[0], SIDE), jnp.bfloat16)
        passed[:, SIDE + col_count :] = jnp.zeros((passed.shape[0], SIDE), jnp.bfloat16)
        build_tables(row_taps, col_taps, rows_ref, cols_ref, laid, row_count, above, runs)
        num_ref[...] = jnp.zeros_like(num_ref)
        if edges:
            source[...] = jnp.zeros_like(source)
        else:
            den_ref[...] = jnp.zeros_like(den_ref)

    @pl.when(covered)
    def _():
        if edges:
            half = top.shape[1]
            source[HALO - half : HALO, :] = top[visit]
            source[HALO : HALO + row_count, :] = images[0]
            source[HALO + row_count : HALO + row_count + half, :] = bottom[visit]
        for b in range(blocks):
            piece = slice(b * BLOCK, (b + 1) * BLOCK)
            data = source[:, piece] if edges else images[0, :, piece]
            out = jnp.dot(rows_ref[...], data, preferred_element_type=jnp.float32)
            passed[:, SIDE + b * BLOCK : SIDE + (b + 1) * BLOCK] = out.astype(jnp.bfloat16)
        row_ids = sky * row_count + lax.broadcasted_iota(jnp.int32, (row_count, 128), 0)
        row_coord = pick((2.0 * row_ids.astype(jnp.float32) + 1.0) / total_rows - 1.0)
        col_ids = lax.broadcasted_iota(jnp.int32, (8, col_count), 1)
        col_coord = (2.0 * col_ids.astype(jnp.float32) + 1.0) / col_count - 1.0
        for basis in range(basis_count):
            band = slice(basis * kept, (basis + 1) * kept)
            lhs = jnp.concatenate(
                [passed[band, b * BLOCK : (b + 2) * BLOCK] for b in range(blocks)], axis=0
            )
            image = jnp.dot(lhs, cols_ref[basis], preferred_element_type=jnp.float32)
            row_part = coeffs[basis, 0, order] + coeffs[basis, 2, order] * row_coord
            row_part = jnp.concatenate([row_part, row_part], axis=1)
            col_part = coeffs[basis, 1, order] * col_coord
            for b in range(blocks):
                piece = slice(b * BLOCK, (b + 1) * BLOCK)
                spatial = row_part.reshape(kept // 8, 8, BLOCK) + col_part[None, :, piece]
                term = spatial.reshape(kept, BLOCK) * image[b * kept : (b + 1) * kept]
                matched[:, piece] = term if basis == 0 else matched[:, piece] + term
        shift = dithers[order]
        inside = (col_ids[0:1] >= shift) & (col_ids[0:1] < shift + (col_count - DITHER))
        weight = inv_var[0].astype(jnp.float32) * inside.astype(jnp.float32)
        num_ref[...] += pick(weight) * matched[...]
        if not edges:
            den_ref[...] += weight

    @pl.when(visit == visit_count - 1)
    def _():
        if edges:
            group = lax.axis_index("visit")
            width = outs[0].shape[1]
            for ahead, out_ref in enumerate(outs):
                at = pl.multiple_of(lax.rem(group + ahead, groups) * width, width)
                edge = num_ref[:, pl.ds(at, width)]
                whole = [edge[:INNER], inner[:, pl.ds(at, width)], edge[INNER:]]
                out_ref[...] = jnp.concatenate(whole, axis=0).astype(out_ref.dtype)
        else:
            inner_ref[...] = num_ref[...]
            split_strips(den_ref, outs)


def coadd_call(dithers, depths, coeffs, row_taps, col_taps, images, inv_var, halos, tiles, groups):
    visit_count, row_count, col_count = images.shape
    basis_count = row_taps.shape[0]
    edges = len(halos) > 0
    kept = 2 * INNER if edges else row_count - 2 * INNER
    width = col_count // groups
    slots = row_count + 2 * HALO if edges else row_count
    whole = lambda shape: pl.BlockSpec(shape, lambda v: (0,) * len(shape))
    scalar = pl.BlockSpec(memory_space=pltpu.SMEM)
    by_visit = lambda rows: pl.BlockSpec((1, rows, col_count), lambda v: (v, 0, 0))
    in_specs = [scalar] * 3 + [whole(row_taps.shape)] * 2 + [by_visit(row_count)] * 2
    shapes = [jax.ShapeDtypeStruct((row_count, width), jnp.float32)]
    shapes += [jax.ShapeDtypeStruct((row_count, width), jnp.bfloat16)] * (groups - 1)
    if edges:
        in_specs += [pl.BlockSpec(memory_space=pltpu.VMEM)] * 2 + [whole(halos[2].shape)]
        last = pltpu.VMEM((slots, col_count), jnp.bfloat16)
    else:
        shapes = [jax.ShapeDtypeStruct((kept, col_count), jnp.float32)] + shapes
        last = pltpu.VMEM((row_count, col_count), jnp.float32)
    streams = visit_count * basis_count * (kept * slots + kept * 2 * BLOCK) * 2 * col_count
    return pl.pallas_call(
        lambda *refs: coadd_kernel(
            *refs, total_rows=row_count * tiles, tiles=tiles, edges=edges, groups=groups
        ),
        out_shape=shapes,
        grid=(visit_count,),
        in_specs=in_specs,
        out_specs=[whole(shape.shape) for shape in shapes],
        scratch_shapes=[
            pltpu.VMEM((basis_count * kept, slots), jnp.bfloat16),
            pltpu.VMEM((basis_count, BLOCK + 2 * SIDE, BLOCK), jnp.bfloat16),
            pltpu.VMEM((2, 16, 512), jnp.float32),
            pltpu.VMEM((basis_count * kept, col_count + 2 * SIDE), jnp.bfloat16),
            pltpu.VMEM((kept, col_count), jnp.float32),
            pltpu.VMEM((kept, col_count), jnp.float32),
            last,
        ],
        compiler_params=pltpu.CompilerParams(
            dimension_semantics=("arbitrary",), vmem_limit_bytes=(52 if edges else 61) << 20
        ),
        cost_estimate=pl.CostEstimate(
            flops=streams, bytes_accessed=images.size * 4, transcendentals=0
        ),
        name="coadd_edges" if edges else "coadd_inner",
    )(dithers, depths, coeffs, row_taps, col_taps, images, inv_var, *halos)


def exchange(own, sends, axis):
    groups = len(sends) + 1
    for ahead in sorted(range(1, groups), key=lambda a: -min(a, groups - a)):
        got = lax.ppermute(
            sends[ahead - 1], axis, [(i, (i + ahead) % groups) for i in range(groups)]
        )
        own = own + got.astype(jnp.float32)
    return own


def local(images, inv_var, row_taps, col_taps, coeffs, dithers, depths):
    row_count = images.shape[1]
    tiles = lax.axis_size("sky")
    groups = lax.axis_size("visit")
    top = lax.ppermute(
        images[:, row_count - INNER :], "sky", [(i, i + 1) for i in range(tiles - 1)]
    )
    bottom = lax.ppermute(images[:, :INNER], "sky", [(i + 1, i) for i in range(tiles - 1)])
    given = (dithers, depths, coeffs.transpose(1, 2, 0), row_taps, col_taps, images, inv_var)
    inner, den_own, *den_sends = coadd_call(*given, (), tiles, groups)
    denominator = exchange(den_own, den_sends, "visit")
    num_own, *num_sends = coadd_call(*given, (top, bottom, inner), tiles, groups)
    numerator = exchange(num_own, num_sends, "visit")
    return numerator / (1.0 + denominator)


def solution(mesh):
    placed = (P("visit", "sky", None), P("visit", "sky", None), P(), P(), P(), P(), P("sky"))
    return jax.shard_map(
        local, mesh=mesh, in_specs=placed, out_specs=P("sky", "visit"), check_vma=False
    )
```

```python
import jax
import jax.numpy as jnp
from jax import lax
from jax.experimental import pallas as pl
from jax.experimental.pallas import tpu as pltpu
from jax.sharding import PartitionSpec as P

DITHER = 256
SIDE = 128
BLOCK = 256
HALO = 32
INNER = 24


def build_tables(row_taps, col_taps, rows_ref, cols_ref, laid, row_count, above, runs):
    basis_count, tap_count = row_taps.shape
    half = tap_count // 2
    kept = rows_ref.shape[0] // basis_count
    nothing = jnp.zeros((128, 128), jnp.bfloat16)
    tap = lax.broadcasted_iota(jnp.int32, (128, 512), 0)
    lane = lax.broadcasted_iota(jnp.int32, (128, 512), 1)
    for which, taps, target in (
        (0, row_taps, lax.rem(above - half + tap + 256, 256)),
        (1, col_taps, SIDE + half - tap),
    ):
        laid[which] = jnp.zeros_like(laid[which])
        laid[which, 0:basis_count, 0:tap_count] = taps[...].astype(jnp.float32)
        picks = ((lane == target) & (tap < tap_count)).astype(jnp.bfloat16)
        laid[which] = jnp.dot(
            laid[which, :, 0:128].astype(jnp.bfloat16), picks, preferred_element_type=jnp.float32
        )

    def step(basis, carry):
        wide = jnp.broadcast_to(laid[0, pl.ds(basis, 1), 0:256], (row_count, 256))
        wide = pltpu.roll(wide, 0, 1, stride=1, stride_axis=0)
        wide = jnp.concatenate([wide[first:last] for first, last in runs], axis=0)
        at = pl.multiple_of(basis * kept, kept)
        rows_ref[pl.ds(at, kept), :] = wide[:, : rows_ref.shape[1]].astype(jnp.bfloat16)
        band = jnp.broadcast_to(laid[1, pl.ds(basis, 1), :], (128, 512))
        band = pltpu.roll(band, 0, 1, stride=1, stride_axis=0).astype(jnp.bfloat16)
        for p in range(cols_ref.shape[1] // 128):
            for x in range(cols_ref.shape[2] // 128):
                apart = p - x
                piece = band[:, (2 - apart) * 128 : (3 - apart) * 128] if 0 <= apart < 3 else nothing
                cols_ref[basis, p * 128 : (p + 1) * 128, x * 128 : (x + 1) * 128] = piece
        return carry

    lax.fori_loop(0, basis_count, step, 0)


def split_strips(total, out_refs):
    groups = len(out_refs)
    width = out_refs[0].shape[1]
    group = lax.axis_index("visit")
    for ahead, out_ref in enumerate(out_refs):
        at = pl.multiple_of(lax.rem(group + ahead, groups) * width, width)
        out_ref[...] = total[:, pl.ds(at, width)].astype(out_ref.dtype)


def coadd_kernel(dithers, depths, coeffs, row_taps, col_taps, images, inv_var, *rest, total_rows, tiles, edges, groups):
    visit = pl.program_id(0)
    visit_count = pl.num_programs(0)
    row_count, col_count = images.shape[1:]
    basis_count = row_taps.shape[0]
    blocks = col_count // BLOCK
    visits_all = dithers.shape[0]
    sky = lax.axis_index("sky")
    order = lax.axis_index("visit") * visit_count + visit
    covered = lax.rem(order - sky * visits_all // tiles + visits_all, visits_all) < depths[0]
    if edges:
        top, bottom, inner = rest[:3]
        outs, (rows_ref, cols_ref, laid, passed, matched, num_ref, source) = (
            rest[3 : 3 + groups],
            rest[3 + groups :],
        )
        runs = ((0, INNER), (row_count - INNER, row_count))
        above = HALO
    else:
        inner_ref = rest[0]
        outs, (rows_ref, cols_ref, laid, passed, matched, num_ref, den_ref) = (
            rest[1 : 1 + groups],
            rest[1 + groups :],
        )
        runs = ((INNER, row_count - INNER),)
        above = 0
    kept = sum(last - first for first, last in runs)

    def pick(value):
        return jnp.concatenate([value[first:last] for first, last in runs], axis=0)

    @pl.when(visit == 0)
    def _():
        passed[:, 0:SIDE] = jnp.zeros((passed.shape[0], SIDE), jnp.bfloat16)
        passed[:, SIDE + col_count :] = jnp.zeros((passed.shape[0], SIDE), jnp.bfloat16)
        build_tables(row_taps, col_taps, rows_ref, cols_ref, laid, row_count, above, runs)
        num_ref[...] = jnp.zeros_like(num_ref)
        if edges:
            source[...] = jnp.zeros_like(source)
        else:
            den_ref[...] = jnp.zeros_like(den_ref)

    @pl.when(covered)
    def _():
        if edges:
            half = top.shape[1]
            source[HALO - half : HALO, :] = top[visit]
            source[HALO : HALO + row_count, :] = images[0]
            source[HALO + row_count : HALO + row_count + half, :] = bottom[visit]
        for b in range(blocks):
            piece = slice(b * BLOCK, (b + 1) * BLOCK)
            data = source[:, piece] if edges else images[0, :, piece]
            out = jnp.dot(rows_ref[...], data, preferred_element_type=jnp.float32)
            passed[:, SIDE + b * BLOCK : SIDE + (b + 1) * BLOCK] = out.astype(jnp.bfloat16)
        row_ids = sky * row_count + lax.broadcasted_iota(jnp.int32, (row_count, 128), 0)
        row_coord = pick((2.0 * row_ids.astype(jnp.float32) + 1.0) / total_rows - 1.0)
        col_ids = lax.broadcasted_iota(jnp.int32, (8, col_count), 1)
        col_coord = (2.0 * col_ids.astype(jnp.float32) + 1.0) / col_count - 1.0
        for basis in range(basis_count):
            band = slice(basis * kept, (basis + 1) * kept)
            lhs = jnp.concatenate(
                [passed[band, b * BLOCK : (b + 2) * BLOCK] for b in range(blocks)], axis=0
            )
            image = jnp.dot(lhs, cols_ref[basis], preferred_element_type=jnp.float32)
            row_part = coeffs[basis, 0, order] + coeffs[basis, 2, order] * row_coord
            row_part = jnp.concatenate([row_part, row_part], axis=1)
            col_part = coeffs[basis, 1, order] * col_coord
            for b in range(blocks):
                piece = slice(b * BLOCK, (b + 1) * BLOCK)
                spatial = row_part.reshape(kept // 8, 8, BLOCK) + col_part[None, :, piece]
                term = spatial.reshape(kept, BLOCK) * image[b * kept : (b + 1) * kept]
                matched[:, piece] = term if basis == 0 else matched[:, piece] + term
        shift = dithers[order]
        inside = (col_ids[0:1] >= shift) & (col_ids[0:1] < shift + (col_count - DITHER))
        weight = inv_var[0].astype(jnp.float32) * inside.astype(jnp.float32)
        num_ref[...] += pick(weight) * matched[...]
        if not edges:
            den_ref[...] += weight

    @pl.when(visit == visit_count - 1)
    def _():
        if edges:
            group = lax.axis_index("visit")
            width = outs[0].shape[1]
            for ahead, out_ref in enumerate(outs):
                at = pl.multiple_of(lax.rem(group + ahead, groups) * width, width)
                edge = num_ref[:, pl.ds(at, width)]
                whole = [edge[:INNER], inner[:, pl.ds(at, width)], edge[INNER:]]
                out_ref[...] = jnp.concatenate(whole, axis=0).astype(out_ref.dtype)
        else:
            inner_ref[...] = num_ref[...]
            split_strips(den_ref, outs)


def coadd_call(dithers, depths, coeffs, row_taps, col_taps, images, inv_var, halos, tiles, groups):
    visit_count, row_count, col_count = images.shape
    basis_count = row_taps.shape[0]
    edges = len(halos) > 0
    kept = 2 * INNER if edges else row_count - 2 * INNER
    width = col_count // groups
    slots = row_count + 2 * HALO if edges else row_count
    whole = lambda shape: pl.BlockSpec(shape, lambda v: (0,) * len(shape))
    scalar = pl.BlockSpec(memory_space=pltpu.SMEM)
    by_visit = lambda rows: pl.BlockSpec((1, rows, col_count), lambda v: (v, 0, 0))
    in_specs = [scalar] * 3 + [whole(row_taps.shape)] * 2 + [by_visit(row_count)] * 2
    shapes = [jax.ShapeDtypeStruct((row_count, width), jnp.float32)]
    shapes += [jax.ShapeDtypeStruct((row_count, width), jnp.bfloat16)] * (groups - 1)
    if edges:
        in_specs += [pl.BlockSpec(memory_space=pltpu.VMEM)] * 2 + [whole(halos[2].shape)]
        last = pltpu.VMEM((slots, col_count), jnp.bfloat16)
    else:
        shapes = [jax.ShapeDtypeStruct((kept, col_count), jnp.float32)] + shapes
        last = pltpu.VMEM((row_count, col_count), jnp.float32)
    streams = visit_count * basis_count * (kept * slots + kept * 2 * BLOCK) * 2 * col_count
    return pl.pallas_call(
        lambda *refs: coadd_kernel(
            *refs, total_rows=row_count * tiles, tiles=tiles, edges=edges, groups=groups
        ),
        out_shape=shapes,
        grid=(visit_count,),
        in_specs=in_specs,
        out_specs=[whole(shape.shape) for shape in shapes],
        scratch_shapes=[
            pltpu.VMEM((basis_count * kept, slots), jnp.bfloat16),
            pltpu.VMEM((basis_count, BLOCK + 2 * SIDE, BLOCK), jnp.bfloat16),
            pltpu.VMEM((2, 16, 512), jnp.float32),
            pltpu.VMEM((basis_count * kept, col_count + 2 * SIDE), jnp.bfloat16),
            pltpu.VMEM((kept, col_count), jnp.float32),
            pltpu.VMEM((kept, col_count), jnp.float32),
            last,
        ],
        compiler_params=pltpu.CompilerParams(
            dimension_semantics=("arbitrary",), vmem_limit_bytes=(52 if edges else 61) << 20
        ),
        cost_estimate=pl.CostEstimate(
            flops=streams, bytes_accessed=images.size * 4, transcendentals=0
        ),
        name="coadd_edges" if edges else "coadd_inner",
    )(dithers, depths, coeffs, row_taps, col_taps, images, inv_var, *halos)


def exchange(own, sends, axis):
    groups = len(sends) + 1
    for ahead in range(1, groups):
        got = lax.ppermute(
            sends[ahead - 1], axis, [(i, (i + ahead) % groups) for i in range(groups)]
        )
        own = own + got.astype(jnp.float32)
    return own


def local(images, inv_var, row_taps, col_taps, coeffs, dithers, depths):
    row_count = images.shape[1]
    tiles = lax.axis_size("sky")
    groups = lax.axis_size("visit")
    top = lax.ppermute(
        images[:, row_count - INNER :], "sky", [(i, i + 1) for i in range(tiles - 1)]
    )
    bottom = lax.ppermute(images[:, :INNER], "sky", [(i + 1, i) for i in range(tiles - 1)])
    given = (dithers, depths, coeffs.transpose(1, 2, 0), row_taps, col_taps, images, inv_var)
    inner, den_own, *den_sends = coadd_call(*given, (), tiles, groups)
    denominator = exchange(den_own, den_sends, "visit")
    num_own, *num_sends = coadd_call(*given, (top, bottom, inner), tiles, groups)
    numerator = exchange(num_own, num_sends, "visit")
    return numerator / (1.0 + denominator)


def solution(mesh):
    placed = (P("visit", "sky", None), P("visit", "sky", None), P(), P(), P(), P(), P("sky"))
    return jax.shard_map(
        local, mesh=mesh, in_specs=placed, out_specs=P("sky", "visit"), check_vma=False
    )
```
